32 devices in a mesh: row: 8 (over z, y), col: 4 (over x, core).
Axes of the slice: x: 2, y: 2, z: 4, core: 2. Of those that a mesh axis runs over, the one named last changes fastest.
Arguments:
- water_depth: float32 [512, 512], P('row', 'col'), may hold values from 1 to 2
- discharge: float32 [2, 512, 512], P(None, 'row', 'col'), may hold values from -1.5 to 1.5
- sediment: float32 [4, 512, 512], P(None, 'row', 'col'), may hold values from 0.01 to 0.1
- bed_level: float32 [128, 128], P(('row', 'col')), may hold values from -3 to 3
- cell_map: int32 [512, 512], P('row', 'col'), may hold values from 0 to 2047, as said below
- wet_mask: int32 [512, 512], P('row', 'col'), may hold values 0 or 1
- sediment_params: float32 [3, 4], replicated, may hold values from 0.5 to 2
Outputs:
- depth_out: float32 [512, 512], P('row', 'col')
- discharge_out: float32 [2, 512, 512], P(None, 'row', 'col')
- sediment_out: float32 [4, 512, 512], P(None, 'row', 'col')
- fine_bed: float32 [512, 512], P('row', 'col')
- bed_out: float32 [128, 128], P(('row', 'col'))
- deposit: float32 [4, 128, 128], P(None, ('row', 'col'))
The draws below stay inside these ranges and needn't reach their ends.
Inputs may be any that keep to these rules, and one draw needn't show every extreme that they name: cell_map[i, j] = r * 128 + c with r within 1 of (i % 64) // 4 and 0 <= r < 16, and c within 3 of j // 4.
All inputs are finite; a program needn't handle non-finite values. No bound on the sum of `wet_mask` on one device may be relied on, other than what follows from the above.
Results may differ from the reference program's by a relative error of at most 0.0003.
Values sent between devices are 32-bit elements; how exact they have to be, the bound alone decides.
No kernel may reach another device: no remote copies, remote signals or barrier semaphores. Data moves between devices by JAX's collectives and lax.ppermute only.
A program may use at most 64 MiB of HBM per device.

```python
import math
import jax
import jax.numpy as jnp
from jax import lax

CX = 64
FRACTIONS = 4
SUBSTEPS = 4
NX = 512
NY = 512
NXC = 128
NYC = 128


def draw_cell_map(key, part):
    row_ids = jnp.arange(NX, dtype=jnp.int32)[:, None] % CX
    col_ids = jnp.arange(NY, dtype=jnp.int32)[None, :]
    shift_row = jax.random.randint(jax.random.fold_in(key, 11), (NX, NY), -1, 2, dtype=jnp.int32)
    shift_col = jax.random.randint(jax.random.fold_in(key, 12), (NX, NY), -3, 4, dtype=jnp.int32)
    band_row = jnp.clip(row_ids // 4 + shift_row, 0, CX // 4 - 1)
    coarse_col = jnp.clip(col_ids // 4 + shift_col, 0, NY // 4 - 1)
    return (band_row * (NY // 4) + coarse_col).astype(jnp.int32)


def plant(array, rng, smallest, high):
    index_at = [jax.random.randint(jax.random.fold_in(rng, axis), (), 0, length) for axis, length in enumerate(array.shape)]
    widest = array.shape.index(max(array.shape))
    beside = index_at[:widest] + [(index_at[widest] + 1) % array.shape[widest]] + index_at[widest + 1:]
    return array.at[tuple(index_at)].set(smallest).at[tuple(beside)].set(high)


def level_of(stream_key, shape, split, least, top_value):
    def one(axis_at, shards_of):
        heights = jax.random.uniform(jax.random.fold_in(jax.random.fold_in(stream_key, 6), axis_at), (shards_of,), jnp.float32, least / len(split), top_value / len(split))
        return jnp.repeat(jnp.exp(heights), shape[axis_at] // shards_of).reshape((-1,) + (1,) * (len(shape) - axis_at - 1))

    gain = one(*split[0])
    for cut in split[1:]:
        gain = gain * one(*cut)
    return gain


def noise(own_key, extent, width, reach, shards=(), kind=jnp.bfloat16):
    gain = level_of(own_key, extent, shards, -0.22, 0.18) if shards else 1.0
    drawn = jax.random.normal(own_key, extent, jnp.float32) * width * gain
    return jnp.minimum(jnp.maximum(drawn, -reach), reach).astype(kind)


def setup_inputs(seed: int = 0) -> dict:
    arg_keys = jax.random.split(jax.random.key(seed), 8)
    water_depth = jnp.clip(1.0 + 1.0 * jax.random.uniform(arg_keys[0], (NX, NY), jnp.float32) ** level_of(arg_keys[0], (NX, NY), ((0, 8), (1, 4)), -0.2, 0.2), 1.0, 2.0)
    discharge = noise(arg_keys[1], (2, NX, NY), 0.3, 1.5, ((1, 8), (2, 4)), jnp.float32)
    sediment = jnp.clip(jnp.exp(math.log(0.1) - 2.3025851 * jax.random.uniform(arg_keys[2], (FRACTIONS, NX, NY), jnp.float32) ** level_of(arg_keys[2], (FRACTIONS, NX, NY), ((1, 8), (2, 4)), -0.2, 0.2)), 0.01, 0.1)
    bed_level = noise(arg_keys[3], (NXC, NYC), 0.3, 3.0, ((0, 32),), jnp.float32)
    cell_map = draw_cell_map(jax.random.fold_in(arg_keys[7], 71), 0)
    wet_mask = plant((jax.random.randint(arg_keys[5], (NX, NY), 0, 10) < 9).astype(jnp.int32), jax.random.fold_in(arg_keys[5], 1), 0, 1)
    sediment_params = jnp.clip(jnp.exp(jax.random.uniform(arg_keys[6], (3, FRACTIONS), jnp.float32, math.log(0.5), math.log(2.0))), 0.5, 2.0)
    return {"water_depth": water_depth, "discharge": discharge, "sediment": sediment, "bed_level": bed_level, "cell_map": cell_map, "wet_mask": wet_mask, "sediment_params": sediment_params}


gravity = 1.0
time_step = 0.2
depth_floor = 1.25
drag_coeff = 0.02
settle_base = 0.05
critical_base = 0.05
erode_base = 0.002
exner_factor = 400.0

def minmod(lower_diff, upper_diff):
    return 0.5 * (jnp.sign(lower_diff) + jnp.sign(upper_diff)) * jnp.minimum(jnp.abs(lower_diff), jnp.abs(upper_diff))

def physical(fields, normal):
    depths = fields[0]
    speed = fields[normal] / jnp.maximum(depths, depth_floor)
    fluxes = fields * speed[None]
    fluxes = fluxes.at[normal].add(0.5 * gravity * depths * depths)
    celerity = jnp.abs(speed) + jnp.sqrt(gravity * depths)
    return (fluxes, celerity)

def face_flux(left_state, right_state, normal):
    left_flux, left_wave = physical(left_state, normal)
    right_flux, right_wave = physical(right_state, normal)
    fastest = jnp.maximum(left_wave, right_wave)
    return 0.5 * (left_flux + right_flux) - 0.5 * fastest[None] * (right_state - left_state)

def advance(fields, bed_pad, wet_pad, params):
    center = fields[:, 2:-2, 2:-2]
    along_rows = fields[:, :, 2:-2]
    slopes = minmod(along_rows[:, 1:-1] - along_rows[:, :-2], along_rows[:, 2:] - along_rows[:, 1:-1])
    middle = along_rows[:, 1:-1]
    left_state = (middle + 0.5 * slopes)[:, :-1]
    right_state = (middle - 0.5 * slopes)[:, 1:]
    open_x = wet_pad[1:-2, 2:-2] * wet_pad[2:-1, 2:-2]
    fluxes = face_flux(left_state, right_state, 1) * open_x[None]
    net_x = fluxes[:, 1:] - fluxes[:, :-1]
    along_cols = fields[:, 2:-2, :]
    slopes = minmod(along_cols[:, :, 1:-1] - along_cols[:, :, :-2], along_cols[:, :, 2:] - along_cols[:, :, 1:-1])
    middle = along_cols[:, :, 1:-1]
    left_state = (middle + 0.5 * slopes)[:, :, :-1]
    right_state = (middle - 0.5 * slopes)[:, :, 1:]
    open_y = wet_pad[2:-2, 1:-2] * wet_pad[2:-2, 2:-1]
    fluxes = face_flux(left_state, right_state, 2) * open_y[None]
    net_y = fluxes[:, :, 1:] - fluxes[:, :, :-1]
    depths = center[0]
    floored = jnp.maximum(depths, depth_floor)
    along_x = center[1] / floored
    along_y = center[2] / floored
    velocity_mag = jnp.sqrt(along_x * along_x + along_y * along_y + 1e-06)
    bed_x = 0.5 * (bed_pad[3:-1, 2:-2] - bed_pad[1:-3, 2:-2])
    bed_y = 0.5 * (bed_pad[2:-2, 3:-1] - bed_pad[2:-2, 1:-3])
    source_x = -gravity * depths * bed_x - drag_coeff * velocity_mag * along_x
    source_y = -gravity * depths * bed_y - drag_coeff * velocity_mag * along_y
    settling = settle_base * params[0][:, None, None] * center[3:] / floored[None]
    critical = critical_base * params[1][:, None, None]
    erosion = erode_base * params[2][:, None, None] * jnp.maximum((velocity_mag * velocity_mag)[None] / critical - 1.0, 0.0)
    exchange = settling - erosion
    sources = jnp.concatenate([jnp.zeros_like(depths)[None], source_x[None], source_y[None], -exchange], axis=0)
    wet_center = wet_pad[2:-2, 2:-2][None]
    updated = center + time_step * wet_center * (sources - net_x - net_y)
    return (updated, time_step * wet_center * exchange)

def reference(water_depth, discharge, sediment, bed_level, cell_map, wet_mask, sediment_params):
    coarse_rows, coarse_cols = bed_level.shape
    row_ids = jnp.arange(NX, dtype=jnp.int32)[:, None]
    band_start = row_ids // CX * (CX // 4)
    coarse_index = ((band_start + cell_map // coarse_cols) * coarse_cols + cell_map % coarse_cols).astype(jnp.int32)
    bed_start = bed_level.reshape(-1)[coarse_index]
    wet = wet_mask.astype(jnp.float32)
    fields = jnp.concatenate([water_depth[None], discharge, sediment], axis=0)
    bed_pad = jnp.pad(bed_start, 2)
    wet_pad = jnp.pad(wet, 2)
    exchanged = jnp.zeros((FRACTIONS, NX, NY), jnp.float32)
    for substep in range(SUBSTEPS):
        fields, change = advance(jnp.pad(fields, ((0, 0), (2, 2), (2, 2))), bed_pad, wet_pad, sediment_params)
        exchanged = exchanged + change
    flat_ids = coarse_index.reshape(-1)
    sums = jax.vmap(lambda column: jax.ops.segment_sum(column, flat_ids, num_segments=coarse_rows * coarse_cols))(exchanged.reshape(FRACTIONS, -1))
    deposit = exner_factor / 16.0 * sums.reshape(FRACTIONS, coarse_rows, coarse_cols)
    bed_new = bed_level + lax.optimization_barrier(jnp.sum(deposit, axis=0))
    fine_bed = bed_new.reshape(-1)[coarse_index]
    return (fields[0], fields[1:3], fields[3:], fine_bed, bed_new, deposit)
```

```python
import functools

import jax
import jax.numpy as jnp
from jax import lax
from jax.experimental import pallas as pl
from jax.experimental.pallas import tpu as pltpu
from jax.sharding import PartitionSpec as P

SUBSTEPS = 4
LANES = 128
SUB = 8
RIM = 2 * SUBSTEPS

gravity = 1.0
time_step = 0.2
depth_floor = 1.25
drag_coeff = 0.02
settle_base = 0.05
critical_base = 0.05
erode_base = 0.002
exner_factor = 400.0


def vmem():
    return pl.BlockSpec(memory_space=pltpu.VMEM)


def smem():
    return pl.BlockSpec(memory_space=pltpu.SMEM)


def lane_ids(shape):
    return lax.broadcasted_iota(jnp.int32, shape, len(shape) - 1)


def pick(table, index):
    return jnp.take_along_axis(table, index, axis=1, mode="promise_in_bounds")


def planes_of(depth, flow, mud, wet, cells):
    out = [lambda r: depth[r, :]]
    out += [lambda r, k=k: flow[k, r, :] for k in range(flow.shape[0])]
    out += [lambda r, k=k: mud[k, r, :] for k in range(mud.shape[0])]
    out += [lambda r: wet[r, :].astype(jnp.float32)]
    out += [lambda r: cells[r, :].astype(jnp.float32)]
    return out


def pack_kernel(depth, flow, mud, wet, cells, strip, out):
    rows = depth.shape[0]
    planes = planes_of(depth, flow, mud, wet, cells)
    group = lane_ids((SUB, LANES)) // RIM
    for start in range(0, rows, SUB):
        at = pl.ds(start, SUB)
        low = jnp.zeros((SUB, LANES), jnp.float32)
        high = low
        for p, plane in enumerate(planes):
            x = plane(at)
            low = jnp.where(group == p, pltpu.roll(x, RIM * p, 1) if p else x, low)
            high = jnp.where(group == p, pltpu.roll(x, (RIM * p + RIM) % LANES, 1), high)
        out[at, :] = low
        out[pl.ds(rows + start, SUB), :] = high
    strip_rows = strip.shape[0]
    for chunk in range(strip.shape[1] // LANES):
        out[pl.ds(2 * rows + chunk * strip_rows, strip_rows), :] = strip[
            :, chunk * LANES : (chunk + 1) * LANES
        ]


def spread_rows(frame_ref, block, shift):
    first = SUB + block * (SUB // 4) + shift
    low = jnp.broadcast_to(frame_ref[pl.ds(first, 1), :], (SUB, LANES))
    high = jnp.broadcast_to(frame_ref[pl.ds(first + 1, 1), :], (SUB, LANES))
    sub = lax.broadcasted_iota(jnp.int32, (SUB, LANES), 0)
    return jnp.where(sub < 4, low, high)


def split_cells(cells, band_cols):
    row = jnp.floor((cells + 0.5) * (1.0 / band_cols))
    return row.astype(jnp.int32), (cells - row * band_cols).astype(jnp.int32)


def row_shift_of(cell_row, block):
    sub = lax.broadcasted_iota(jnp.int32, (SUB, LANES), 0)
    return cell_row - (block * (SUB // 4) + sub // 4)


def lookup(frame_ref, block, shift, column):
    found = pick(spread_rows(frame_ref, block, 0), column)
    below = pick(spread_rows(frame_ref, block, -1), column)
    above = pick(spread_rows(frame_ref, block, 1), column)
    return jnp.where(shift == 0, found, jnp.where(shift < 0, below, above))


def fill_frame(frame_ref, band_rows, rows_of):
    frame_ref[...] = jnp.zeros_like(frame_ref)
    for r0, value in rows_of:
        frame_ref[pl.ds(SUB + r0, value.shape[0]), :] = value


def mid_kernel(
    geometry, depth, flow, mud, wet, cells, packs, frame, place,
    side, bed, code, send_a, send_b, frame_ref,
):
    rows = depth.shape[0]
    fractions = mud.shape[0]
    band_cols, cols_count, strip_rows, from_packs = geometry
    row_at, col_at, frame_start = place[0], place[1], place[2]
    coarse_start = place[3]
    if from_packs:
        fill_frame(
            frame_ref, None,
            [(d * strip_rows, packs[d, pl.ds(2 * rows, strip_rows), :]) for d in range(cols_count)],
        )
    else:
        fill_frame(frame_ref, None, [(0, frame[...])])
    lane = lane_ids((SUB, LANES))
    width = 4 * RIM
    inside = lane % width
    group = lane // width
    is_low = inside < RIM
    is_high = inside >= 3 * RIM
    own_index = jnp.where(
        is_low | is_high, 0, jnp.where(inside < 2 * RIM, inside - RIM, inside - 2 * RIM + LANES - RIM)
    )
    has_low = jnp.where(col_at > 0, 1.0, 0.0)
    has_high = jnp.where(col_at < cols_count - 1, 1.0, 0.0)
    scale = jnp.where(is_low, has_low, jnp.where(is_high, has_high, 1.0))
    left = jnp.maximum(col_at - 1, 0)
    right = jnp.minimum(col_at + 1, cols_count - 1)
    planes = planes_of(depth, flow, mud, wet, cells)
    count = len(planes)
    wet_at, cell_at = count - 2, count - 1
    parity = row_at % 2
    for block in range(rows // SUB):
        at = pl.ds(block * SUB, SUB)
        from_left = packs[left, pl.ds(rows + block * SUB, SUB), :]
        from_right = packs[right, pl.ds(block * SUB, SUB), :]

        def side_of(own, p):
            index = p * RIM + lane % RIM
            x = jnp.where(is_low, pick(from_left, index), jnp.where(is_high, pick(from_right, index), own))
            return x * scale

        def own_of(p):
            return pick(planes[p](at), own_index)

        sides = [side_of(own_of(p), p) for p in range(3)]
        own = own_of(3)
        for k in range(1, fractions):
            own = jnp.where(group == k, own_of(3 + k), own)
        sides.append(side_of(own, 3 + group))
        sides.append(side_of(own_of(wet_at), wet_at))
        side_row, side_col = split_cells(side_of(own_of(cell_at), cell_at), band_cols)
        side_at = jnp.where(scale > 0.0, side_col - frame_start, 0)
        sides.append(lookup(frame_ref, block, row_shift_of(side_row, block), side_at) * scale)
        cell_row, cell_col = split_cells(cells[at, :].astype(jnp.float32), band_cols)
        shift = row_shift_of(cell_row, block)
        bed_here = lookup(frame_ref, block, shift, cell_col - frame_start)
        bed[at, :] = bed_here
        code[at, :] = (shift + 1) * 7 + (cell_col - coarse_start - lane // 4 + 3)
        for p, x in enumerate(sides):
            side[p, at, :] = x
        edge = [planes[p](at) for p in range(count - 1)] + [bed_here] + sides

        def write(out):
            for p, x in enumerate(edge):
                out[p, :, :] = x

        if block == 0:
            pl.when(parity == 1)(lambda: write(send_a))
            pl.when(parity == 0)(lambda: write(send_b))
        if block == rows // SUB - 1:
            pl.when(parity == 0)(lambda: write(send_a))
            pl.when(parity == 1)(lambda: write(send_b))


def half_minmod(before, here, after):
    low = 0.5 * (here - before)
    high = 0.5 * (after - here)
    return jnp.maximum(jnp.minimum(low, high), jnp.minimum(jnp.maximum(low, high), 0.0))


def face_fluxes(lefts, rights, normal, half_open):
    speed_l = lefts[normal] * pl.reciprocal(jnp.maximum(lefts[0], depth_floor))
    speed_r = rights[normal] * pl.reciprocal(jnp.maximum(rights[0], depth_floor))
    wave = jnp.maximum(
        jnp.abs(speed_l) + jnp.sqrt(gravity * lefts[0]), jnp.abs(speed_r) + jnp.sqrt(gravity * rights[0])
    )
    to_l = half_open * (speed_l + wave)
    to_r = half_open * (speed_r - wave)
    out = [l * to_l + r * to_r for l, r in zip(lefts, rights)]
    out[normal] = out[normal] + (0.5 * gravity) * half_open * (lefts[0] * lefts[0] + rights[0] * rights[0])
    return out


def flow_kernel(
    depth, flow, mud, wet, bed, side, code, params, place, recv_a, recv_b,
    depth_out, flow_out, mud_out, partial,
    q_main, q_side, static_main, static_side, slope_main, slope_side, flux_main, flux_side, exchanged, code_ref,
):
    rows = depth.shape[0]
    fractions = mud.shape[0]
    channels = 3 + fractions
    top = SUB
    body = top + RIM
    blocks = (rows + 2 * RIM) // SUB
    parity = place[0] % 2
    lane = lane_ids((SUB, LANES))
    width = 4 * RIM
    group = lane // width

    main_planes = [depth] + [flow.at[k] for k in range(2)] + [mud.at[k] for k in range(fractions)]
    wet_main, bed_main = 0, 1

    def fill(dst, p_dst, own, p_recv):
        dst[p_dst, pl.ds(body, rows), :] = own
        a, b = recv_a[p_recv], recv_b[p_recv]
        dst[p_dst, pl.ds(top, RIM), :] = jnp.where(parity == 1, a, b)
        dst[p_dst, pl.ds(body + rows, RIM), :] = jnp.where(parity == 1, b, a)

    for k in range(channels):
        fill(q_main.at[0], k, main_planes[k][...], k)
    fill(static_main, wet_main, wet[...].astype(jnp.float32), channels)
    fill(static_main, bed_main, bed[...], channels + 1)
    for k in range(4):
        fill(q_side.at[0], k, side[k], channels + 2 + k)
    fill(static_side, wet_main, side[4], channels + 6)
    fill(static_side, bed_main, side[5], channels + 7)

    settle = [[settle_base * params[0, k] for k in range(fractions)]]
    inv_crit = [[1.0 / (critical_base * params[1, k]) for k in range(fractions)]]
    erode = [[erode_base * params[2, k] for k in range(fractions)]]

    def by_group(values):
        out = jnp.full((SUB, LANES), values[0], jnp.float32)
        for k in range(1, fractions):
            out = jnp.where(group == k, values[k], out)
        return out

    side_coeffs = ([by_group(settle[0])], [by_group(inv_crit[0])], [by_group(erode[0])])
    main_coeffs = (settle[0], inv_crit[0], erode[0])

    def edge_fix(k):
        g = (k - 3) if k >= 3 else 0
        return jnp.where(lane == 0, g * width + RIM - 1, jnp.where(lane == LANES - 1, g * width + 3 * RIM, 0))

    def flux_fix(k):
        g = (k - 3) if k >= 3 else 0
        return jnp.where(lane == 0, g * width + RIM - 1, jnp.where(lane == LANES - 1, g * width + 3 * RIM - 1, 0))

    edge_index = [edge_fix(max(k, 3)) for k in range(3, 3 + fractions)]
    flux_index = [flux_fix(max(k, 3)) for k in range(3, 3 + fractions)]
    first_lane = lane == 0
    last_lane = lane == LANES - 1

    def rows_at(ref, p, row):
        return ref[p, pl.ds(row, SUB), :]

    def statics(block, carry):
        r0 = pl.multiple_of(top + block * SUB, SUB)
        for ref, is_main in ((static_side, False), (static_main, True)):
            w = rows_at(ref, wet_main, r0)
            b_plus = rows_at(ref, bed_main, r0 + 1)
            b_minus = rows_at(ref, bed_main, r0 - 1)
            b = rows_at(ref, bed_main, r0)
            w_right, b_right = pltpu.roll(w, LANES - 1, 1), pltpu.roll(b, LANES - 1, 1)
            b_left = pltpu.roll(b, 1, 1)
            if is_main:
                w_edge = pick(rows_at(static_side, wet_main, r0), edge_index[0])
                b_edge = pick(rows_at(static_side, bed_main, r0), edge_index[0])
                w_right = jnp.where(last_lane, w_edge, w_right)
                b_right = jnp.where(last_lane, b_edge, b_right)
                b_left = jnp.where(first_lane, b_edge, b_left)
            at = pl.ds(r0, SUB)
            ref[2, at, :] = 0.5 * (w * rows_at(ref, wet_main, r0 + 1))
            ref[3, at, :] = 0.5 * (w * w_right)
            ref[4, at, :] = (0.5 * gravity) * (b_plus - b_minus)
            ref[5, at, :] = (0.5 * gravity) * (b_right - b_left)
            ref[6, at, :] = time_step * w
        return carry

    lax.fori_loop(0, blocks, statics, 0)

    def slopes(block, level):
        r0 = pl.multiple_of(top + block * SUB, SUB)
        at = pl.ds(r0, SUB)
        for q, s, n in ((q_side, slope_side, 4), (q_main, slope_main, channels)):
            if n == 4 and level == SUBSTEPS - 1:
                continue
            q = q.at[level % 2]
            for k in range(n):
                s[k, at, :] = half_minmod(rows_at(q, k, r0 - 1), rows_at(q, k, r0), rows_at(q, k, r0 + 1))

    def row_fluxes(q, s, f, static, n, r0):
        lefts = [rows_at(q, k, r0) + rows_at(s, k, r0) for k in range(n)]
        rights = [rows_at(q, k, r0 + 1) - rows_at(s, k, r0 + 1) for k in range(n)]
        out = face_fluxes(lefts, rights, 1, rows_at(static, 2, r0))
        for k in range(n):
            f[k, pl.ds(r0, SUB), :] = out[k]
        return [rows_at(f, k, r0 - 1) - out[k] for k in range(n)]

    def col_fluxes(here, static, n, r0, edges):
        lefts, rights = [], []
        for k in range(n):
            before, after = pltpu.roll(here[k], 1, 1), pltpu.roll(here[k], LANES - 1, 1)
            if edges is not None:
                edge = pick(edges[min(k, 3)], edge_index[max(k - 3, 0)])
                before = jnp.where(first_lane, edge, before)
                after = jnp.where(last_lane, edge, after)
            s = half_minmod(before, here[k], after)
            lefts.append(here[k] + s)
            rights.append(pltpu.roll(here[k] - s, LANES - 1, 1))
        return face_fluxes(lefts, rights, 2, rows_at(static, 3, r0))

    def update(here, net, static, coeffs, r0):
        step = rows_at(static, 6, r0)
        inv = pl.reciprocal(jnp.maximum(here[0], depth_floor))
        u, v = here[1] * inv, here[2] * inv
        squared = u * u + v * v + 1e-06
        drag = drag_coeff * jnp.sqrt(squared)
        new = [
            here[0] + step * net[0],
            here[1] + step * (net[1] - here[0] * rows_at(static, 4, r0) - drag * u),
            here[2] + step * (net[2] - here[0] * rows_at(static, 5, r0) - drag * v),
        ]
        changes = []
        for k in range(len(here) - 3):
            m = here[3 + k]
            settled = coeffs[0][k] * m * inv
            eroded = coeffs[2][k] * jnp.maximum(squared * coeffs[1][k] - 1.0, 0.0)
            change = step * (settled - eroded)
            changes.append(change)
            new.append(m + step * net[3 + k] - change)
        return new, changes

    def advance(block, level, rows_only=False):
        r0 = pl.multiple_of(top + block * SUB, SUB)
        at = pl.ds(r0, SUB)
        last = level == SUBSTEPS - 1
        qs, qm = q_side.at[level % 2], q_main.at[level % 2]
        if rows_only:
            row_fluxes(qm, slope_main, flux_main, static_main, channels, r0)
            return
        edges = [rows_at(qs, k, r0) for k in range(4)]
        side_flux = col_fluxes(edges, static_side, 4, r0, None)
        if not last:
            net = row_fluxes(qs, slope_side, flux_side, static_side, 4, r0)
            net = [x + (pltpu.roll(f, 1, 1) - f) for x, f in zip(net, side_flux)]
            new, _ = update(edges, net, static_side, side_coeffs, r0)
            for k in range(4):
                q_side[(level + 1) % 2, k, at, :] = new[k]
        net = row_fluxes(qm, slope_main, flux_main, static_main, channels, r0)
        here = [rows_at(qm, k, r0) for k in range(channels)]
        fluxes = col_fluxes(here, static_main, channels, r0, edges)
        for k in range(channels):
            edge = pick(side_flux[min(k, 3)], flux_index[max(k - 3, 0)])
            f = jnp.where(last_lane, edge, fluxes[k])
            net[k] = net[k] + (jnp.where(first_lane, edge, pltpu.roll(fluxes[k], 1, 1)) - f)
        new, changes = update(here, net, static_main, main_coeffs, r0)
        if last:
            out = pl.ds(pl.multiple_of(r0 - body, SUB), SUB)
            depth_out[out, :] = new[0]
            flow_out[0, out, :] = new[1]
            flow_out[1, out, :] = new[2]
            for k in range(fractions):
                mud_out[k, out, :] = new[3 + k]
        else:
            for k in range(channels):
                q_main[(level + 1) % 2, k, at, :] = new[k]
        for k in range(fractions):
            if level == 0:
                exchanged[k, at, :] = changes[k]
            else:
                exchanged[k, at, :] = exchanged[k, at, :] + changes[k]

    for level in range(SUBSTEPS):
        last = level == SUBSTEPS - 1

        def slope_step(block, carry, level=level):
            slopes(block, level)
            return carry

        def advance_step(block, carry, level=level):
            advance(block, level)
            return carry

        lax.fori_loop(0, blocks, slope_step, 0)
        if last:
            advance(0, level, rows_only=True)
            lax.fori_loop(1, blocks - 1, advance_step, 0)
        else:
            lax.fori_loop(0, blocks, advance_step, 0)

    coarse_rows = rows // 4
    code_ref[...] = code[...]
    parts = [[exchanged[f, pl.ds(body + k, coarse_rows, stride=4), :] for k in range(4)] for f in range(fractions)]
    codes = [code_ref[pl.ds(k, coarse_rows, stride=4), :] for k in range(4)]
    to_coarse = (
        lax.broadcasted_iota(jnp.int32, (LANES, LANES), 0) // 4 == lax.broadcasted_iota(jnp.int32, (LANES, LANES), 1)
    ).astype(jnp.float32)
    total = None
    for col_shift in range(7):
        sums = [None] * fractions
        for row_shift in range(3):
            hits = [c == row_shift * 7 + col_shift for c in codes]
            for f in range(fractions):
                part = None
                for k in range(4):
                    x = jnp.where(hits[k], parts[f][k], 0.0)
                    part = x if part is None else part + x
                if row_shift != 1:
                    part = pltpu.roll(part, 1 if row_shift == 2 else coarse_rows - 1, 0)
                sums[f] = part if sums[f] is None else sums[f] + part
        z = jnp.dot(
            jnp.concatenate(sums, axis=0), to_coarse, precision=lax.Precision.HIGHEST,
            preferred_element_type=jnp.float32,
        )
        z = pltpu.roll(z, (place[3] - place[2] + col_shift - 3 + LANES) % LANES, 1)
        total = z if total is None else total + z
    partial[...] = total


def bed_kernel(geometry, sums, bed, cells, place, bed_out, deposit_out, fine, frame_ref, total_ref):
    band_cols, cols_count, strip_rows = geometry
    rows = cells.shape[0]
    band_rows = rows // 4
    fractions = sums.shape[1] // band_rows
    total = sums[0]
    for d in range(1, cols_count):
        total = total + sums[d]
    total_ref[...] = (exner_factor / 16.0) * total
    at = place[1] * strip_rows
    frame_ref[...] = jnp.zeros_like(frame_ref)
    whole = None
    for f in range(fractions):
        part = total_ref[pl.ds(f * band_rows, band_rows), :]
        whole = part if whole is None else whole + part
        deposit_out[f, :, :] = total_ref[pl.ds(f * band_rows + at, strip_rows), :]
    frame_ref[pl.ds(SUB, band_rows), :] = bed[pl.ds(SUB, band_rows), :] + whole
    bed_out[...] = frame_ref[pl.ds(SUB + at, strip_rows), :]
    for block in range(rows // SUB):
        here = pl.ds(block * SUB, SUB)
        cell_row, cell_col = split_cells(cells[here, :].astype(jnp.float32), band_cols)
        fine[here, :] = lookup(frame_ref, block, row_shift_of(cell_row, block), cell_col)


def local(water_depth, discharge, sediment, bed_level, cell_map, wet_mask, sediment_params):
    tile_rows, tile_cols = water_depth.shape
    fractions = sediment.shape[0]
    strip_rows, band_cols = bed_level.shape
    cols_count = lax.axis_size("col")
    rows_count = lax.axis_size("row")
    band_rows = tile_rows // 4
    f32 = functools.partial(jax.ShapeDtypeStruct, dtype=jnp.float32)
    row_at, col_at = lax.axis_index("row"), lax.axis_index("col")
    coarse_start = col_at * (tile_cols // 4)
    narrow = band_cols == LANES
    frame_start = 0 * coarse_start if narrow else coarse_start - (LANES - tile_cols // 4) // 2
    place = jnp.stack([row_at, col_at, frame_start, coarse_start]).astype(jnp.int32)
    chunks = band_cols // LANES
    pack_rows = 2 * tile_rows + -(-chunks * strip_rows // SUB) * SUB

    packed = pl.pallas_call(
        pack_kernel, out_shape=f32((pack_rows, LANES)), in_specs=[vmem()] * 6, out_specs=vmem(),
    )(water_depth, discharge, sediment, wet_mask, cell_map, bed_level)
    packs = lax.all_gather(packed, "col", axis=0)

    if narrow:
        frame = jnp.zeros((SUB, LANES), jnp.float32)
    else:
        strips = packs[:, 2 * tile_rows : 2 * tile_rows + chunks * strip_rows]
        band = strips.reshape(cols_count, chunks, strip_rows, LANES).transpose(0, 2, 1, 3).reshape(band_rows, band_cols)
        wide = jnp.pad(band, ((0, 0), (LANES, LANES)))
        frame = lax.dynamic_slice(wide, (jnp.int32(0), frame_start + LANES), (band_rows, LANES))
    edge_planes = 3 + fractions + 2 + 6
    side, bed, code, send_a, send_b, framed = pl.pallas_call(
        functools.partial(mid_kernel, (band_cols, cols_count, strip_rows, narrow)),
        out_shape=(
            f32((6, tile_rows, LANES)), f32((tile_rows, LANES)), jax.ShapeDtypeStruct((tile_rows, LANES), jnp.int32),
            f32((edge_planes, SUB, LANES)), f32((edge_planes, SUB, LANES)), f32((band_rows + 2 * SUB, LANES)),
        ),
        in_specs=[vmem()] * 7 + [smem()], out_specs=(vmem(),) * 6,
    )(water_depth, discharge, sediment, wet_mask, cell_map, packs, frame, place)

    pairs_a = [p for i in range(0, rows_count - 1, 2) for p in ((i, i + 1), (i + 1, i))]
    pairs_b = [p for i in range(1, rows_count - 1, 2) for p in ((i, i + 1), (i + 1, i))]
    recv_a = lax.ppermute(send_a, "row", pairs_a)
    recv_b = lax.ppermute(send_b, "row", pairs_b)

    channels = 3 + fractions
    span = tile_rows + 2 * RIM + 2 * SUB
    space = functools.partial(pltpu.VMEM, dtype=jnp.float32)
    depth_out, discharge_out, sediment_out, partial = pl.pallas_call(
        flow_kernel,
        out_shape=(
            f32(water_depth.shape), f32(discharge.shape), f32(sediment.shape), f32((fractions * band_rows, LANES)),
        ),
        in_specs=[vmem()] * 7 + [smem()] * 2 + [vmem()] * 2, out_specs=(vmem(),) * 4,
        scratch_shapes=[
            space((2, channels, span, LANES)), space((2, 4, span, LANES)), space((7, span, LANES)),
            space((7, span, LANES)), space((channels, span, LANES)), space((4, span, LANES)),
            space((channels, span, LANES)), space((4, span, LANES)), space((fractions, span, LANES)),
            pltpu.VMEM((tile_rows, LANES), jnp.int32),
        ],
    )(water_depth, discharge, sediment, wet_mask, bed, side, code, sediment_params, place, recv_a, recv_b)

    sums = lax.all_gather(partial, "col", axis=0)
    geometry = (band_cols if narrow else LANES, cols_count, strip_rows)
    if narrow:
        look_cells = cell_map
    else:
        wide = jnp.zeros((fractions, band_rows, band_cols + 2 * LANES), jnp.float32)
        for d in range(cols_count):
            start = LANES + d * (tile_cols // 4) - (LANES - tile_cols // 4) // 2
            wide = wide.at[:, :, start : start + LANES].add(sums[d].reshape(fractions, band_rows, LANES))
        share = lax.dynamic_slice_in_dim(wide, col_at * strip_rows, strip_rows, axis=1)[:, :, LANES:-LANES]
        deposit_wide = exner_factor / 16.0 * share
        bed_wide = bed_level + jnp.sum(deposit_wide, axis=0)
        sums = lax.dynamic_slice_in_dim(wide, frame_start + LANES, LANES, axis=2).reshape(1, -1, LANES)
        geometry = (LANES, 1, strip_rows)
        look_cells = cell_map // band_cols * LANES + cell_map % band_cols - frame_start
    bed_new, deposit, fine_bed = pl.pallas_call(
        functools.partial(bed_kernel, geometry),
        out_shape=(f32((strip_rows, LANES)), f32((fractions, strip_rows, LANES)), f32((tile_rows, LANES))),
        in_specs=[vmem()] * 3 + [smem()], out_specs=(vmem(),) * 3,
        scratch_shapes=[space((band_rows + 2 * SUB, LANES)), space((fractions * band_rows, LANES))],
    )(sums, framed, look_cells, place)
    if not narrow:
        bed_new, deposit = bed_wide, deposit_wide
    return (depth_out, discharge_out, sediment_out, fine_bed, bed_new, deposit)


def solution(mesh):
    placed = (
        P("row", "col"),
        P(None, "row", "col"),
        P(None, "row", "col"),
        P(("row", "col"), None),
        P("row", "col"),
        P("row", "col"),
        P(),
    )
    return jax.shard_map(
        local,
        mesh=mesh,
        in_specs=placed,
        out_specs=(
            P("row", "col"),
            P(None, "row", "col"),
            P(None, "row", "col"),
            P("row", "col"),
            P(("row", "col"), None),
            P(None, ("row", "col"), None),
        ),
        check_vma=False,
    )
```

```python
import functools

import jax
import jax.numpy as jnp
from jax import lax
from jax.experimental import pallas as pl
from jax.experimental.pallas import tpu as pltpu
from jax.sharding import PartitionSpec as P

SUBSTEPS = 4
LANES = 128
SUB = 8
UNROLL = 2
RIM = 2 * SUBSTEPS

gravity = 1.0
time_step = 0.2
depth_floor = 1.25
drag_coeff = 0.02
settle_base = 0.05
critical_base = 0.05
erode_base = 0.002
exner_factor = 400.0


def vmem():
    return pl.BlockSpec(memory_space=pltpu.VMEM)


def smem():
    return pl.BlockSpec(memory_space=pltpu.SMEM)


def lane_ids(shape):
    return lax.broadcasted_iota(jnp.int32, shape, len(shape) - 1)


def params_of(limit=16 << 20):
    return pltpu.CompilerParams(vmem_limit_bytes=limit)


def pick(table, index):
    return jnp.take_along_axis(table, index, axis=1, mode="promise_in_bounds")


def planes_of(depth, flow, mud, wet, cells):
    out = [lambda r: depth[r, :]]
    out += [lambda r, k=k: flow[k, r, :] for k in range(flow.shape[0])]
    out += [lambda r, k=k: mud[k, r, :] for k in range(mud.shape[0])]
    out += [lambda r: wet[r, :].astype(jnp.float32)]
    out += [lambda r: cells[r, :].astype(jnp.float32)]
    return out


def folded_rows(rows):
    return -(-rows // SUB // (LANES // (2 * RIM)))


def pack_kernel(depth, flow, mud, wet, cells, strip, out):
    rows = depth.shape[0]
    planes = planes_of(depth, flow, mud, wet, cells)
    group = lane_ids((SUB, LANES)) // RIM
    pairs = LANES // (2 * RIM)
    spare = [[None] * folded_rows(rows) for _ in planes[pairs:]]
    for block in range(rows // SUB):
        at = pl.ds(block * SUB, SUB)
        packed = None
        for p, plane in enumerate(planes):
            x = plane(at)
            slot = p if p < pairs else block % pairs
            low = pltpu.roll(x, 2 * RIM * slot, 1) if slot else x
            high = pltpu.roll(x, (2 * RIM * slot + 2 * RIM) % LANES, 1)
            old = packed if p < pairs else spare[p - pairs][block // pairs]
            both = jnp.where(group == 2 * slot, low, high)
            new = both if old is None else jnp.where(group // 2 == slot, both, old)
            if p < pairs:
                packed = new
            else:
                spare[p - pairs][block // pairs] = new
        out[at, :] = packed
    start = rows
    for x in [x for p in spare for x in p]:
        out[pl.ds(start, SUB), :] = x
        start += SUB
    strip_rows = strip.shape[0]
    for chunk in range(strip.shape[1] // LANES):
        out[pl.ds(start + chunk * strip_rows, strip_rows), :] = strip[:, chunk * LANES : (chunk + 1) * LANES]


def spread_rows(frame_ref, block, shift):
    first = SUB + block * (SUB // 4) + shift
    low = jnp.broadcast_to(frame_ref[pl.ds(first, 1), :], (SUB, LANES))
    high = jnp.broadcast_to(frame_ref[pl.ds(first + 1, 1), :], (SUB, LANES))
    sub = lax.broadcasted_iota(jnp.int32, (SUB, LANES), 0)
    return jnp.where(sub < 4, low, high)


def split_cells(cells, band_cols):
    row = jnp.floor((cells + 0.5) * (1.0 / band_cols))
    return row.astype(jnp.int32), (cells - row * band_cols).astype(jnp.int32)


def row_shift_of(cell_row, block):
    sub = lax.broadcasted_iota(jnp.int32, (SUB, LANES), 0)
    return cell_row - (block * (SUB // 4) + sub // 4)


def lookup(frame_ref, block, shift, column):
    found = pick(spread_rows(frame_ref, block, 0), column)
    below = pick(spread_rows(frame_ref, block, -1), column)
    above = pick(spread_rows(frame_ref, block, 1), column)
    return jnp.where(shift == 0, found, jnp.where(shift < 0, below, above))


def starts_of(col_at, band_cols):
    coarse_start = col_at * (LANES // 4)
    return coarse_start, 0 if band_cols == LANES else coarse_start - (LANES - LANES // 4) // 2


def fill_frame(frame_ref, rows_of):
    frame_ref[...] = jnp.zeros_like(frame_ref)
    for r0, value in rows_of:
        frame_ref[pl.ds(SUB + r0, value.shape[0]), :] = value


def mid_kernel(
    geometry, depth, flow, mud, wet, cells, packs, *refs
):
    band_cols, cols_count, strip_rows, from_packs = geometry
    frame = None if from_packs else refs[0]
    side, bed, code, send_a, send_b, frame_ref = refs[0 if from_packs else 1 :]
    rows = depth.shape[0]
    fractions = mud.shape[0]
    row_at, col_at = lax.axis_index("row"), lax.axis_index("col")
    coarse_start, frame_start = starts_of(col_at, band_cols)
    planes = planes_of(depth, flow, mud, wet, cells)
    count = len(planes)
    wet_at, cell_at = count - 2, count - 1
    pairs = LANES // (2 * RIM)
    strip_at = rows + (count - pairs) * folded_rows(rows) * SUB
    if from_packs:
        fill_frame(
            frame_ref,
            [(d * strip_rows, packs[d, pl.ds(strip_at, strip_rows), :]) for d in range(cols_count)],
        )
    else:
        fill_frame(frame_ref, [(0, frame[...])])
    lane = lane_ids((SUB, LANES))
    width = 4 * RIM
    inside = lane % width
    group = lane // width
    is_low = inside < RIM
    is_high = inside >= 3 * RIM
    is_first = inside < 2 * RIM
    has_low = jnp.where(col_at > 0, 1.0, 0.0)
    has_high = jnp.where(col_at < cols_count - 1, 1.0, 0.0)
    scale = jnp.where(is_low, has_low, jnp.where(is_high, has_high, 1.0))
    left = jnp.maximum(col_at - 1, 0)
    right = jnp.minimum(col_at + 1, cols_count - 1)
    parity = row_at % 2

    def turn(x, shift):
        shift = shift % LANES
        return pltpu.roll(x, shift, 1) if shift else x

    for block in range(rows // SUB):
        at = pl.ds(block * SUB, SUB)

        def gather_to(p, base):
            if p < pairs:
                source, slot = at, p
            else:
                source = pl.ds(rows + ((p - pairs) * folded_rows(rows) + block // pairs) * SUB, SUB)
                slot = block % pairs
            x = planes[p](at)
            low = turn(packs[left, source, :], base - 2 * RIM * slot - RIM)
            high = turn(packs[right, source, :], base + 3 * RIM - 2 * RIM * slot)
            own = jnp.where(is_first, turn(x, base + RIM), turn(x, base + 3 * RIM))
            return jnp.where(is_low, low, jnp.where(is_high, high, own))

        def for_all(p):
            x = gather_to(p, 0)
            x = jnp.where(lane < width, x, pltpu.roll(x, width, 1))
            return jnp.where(lane < 2 * width, x, pltpu.roll(x, 2 * width, 1)) * scale

        sides = [for_all(p) for p in range(3)]
        each = gather_to(3, 0)
        for k in range(1, fractions):
            each = jnp.where(group == k, gather_to(3 + k, k * width), each)
        sides.append(each * scale)
        sides.append(for_all(wet_at))
        side_row, side_col = split_cells(for_all(cell_at), band_cols)
        side_at = jnp.where(scale > 0.0, side_col - frame_start, 0)
        sides.append(lookup(frame_ref, block, row_shift_of(side_row, block), side_at) * scale)
        cell_row, cell_col = split_cells(cells[at, :].astype(jnp.float32), band_cols)
        shift = row_shift_of(cell_row, block)
        bed_here = lookup(frame_ref, block, shift, cell_col - frame_start)
        bed[at, :] = bed_here
        code[at, :] = (shift + 1) * 7 + (cell_col - coarse_start - lane // 4 + 3)
        for p, x in enumerate(sides):
            side[p, at, :] = x
        edge = [planes[p](at) for p in range(count - 1)] + [bed_here] + sides

        def write(out):
            for p, x in enumerate(edge):
                out[p, :, :] = x

        if block == 0:
            pl.when(parity == 1)(lambda: write(send_a))
            pl.when(parity == 0)(lambda: write(send_b))
        if block == rows // SUB - 1:
            pl.when(parity == 0)(lambda: write(send_a))
            pl.when(parity == 1)(lambda: write(send_b))


def half_minmod(before, here, after):
    low = 0.5 * (here - before)
    high = 0.5 * (after - here)
    return jnp.maximum(jnp.minimum(low, high), jnp.minimum(jnp.maximum(low, high), 0.0))


def face_fluxes(lefts, rights, normal, half_open):
    speed_l = lefts[normal] * pl.reciprocal(jnp.maximum(lefts[0], depth_floor))
    speed_r = rights[normal] * pl.reciprocal(jnp.maximum(rights[0], depth_floor))
    wave = jnp.maximum(
        jnp.abs(speed_l) + jnp.sqrt(gravity * lefts[0]), jnp.abs(speed_r) + jnp.sqrt(gravity * rights[0])
    )
    to_l = half_open * (speed_l + wave)
    to_r = half_open * (speed_r - wave)
    out = [l * to_l + r * to_r for l, r in zip(lefts, rights)]
    out[normal] = out[normal] + (0.5 * gravity) * half_open * (lefts[0] * lefts[0] + rights[0] * rights[0])
    return out


def flow_kernel(
    band_cols, depth, flow, mud, wet, bed, side, code, params, recv_a, recv_b,
    depth_out, flow_out, mud_out, partial,
    q_main, q_side, static_main, static_side, slope_main, slope_side, flux_main, flux_side, exchanged, code_ref,
):
    rows = depth.shape[0]
    fractions = mud.shape[0]
    channels = 3 + fractions
    top = SUB
    body = top + RIM
    blocks = (rows + 2 * RIM) // SUB
    parity = lax.axis_index("row") % 2
    lane = lane_ids((SUB, LANES))
    width = 4 * RIM
    group = lane // width

    main_planes = [depth] + [flow.at[k] for k in range(2)] + [mud.at[k] for k in range(fractions)]
    wet_main, bed_main = 0, 1

    def fill(dst, p_dst, own, p_recv):
        dst[p_dst, pl.ds(body, rows), :] = own
        a, b = recv_a[p_recv], recv_b[p_recv]
        dst[p_dst, pl.ds(top, RIM), :] = jnp.where(parity == 1, a, b)
        dst[p_dst, pl.ds(body + rows, RIM), :] = jnp.where(parity == 1, b, a)

    for k in range(channels):
        fill(q_main.at[0], k, main_planes[k][...], k)
    fill(static_main, wet_main, wet[...].astype(jnp.float32), channels)
    fill(static_main, bed_main, bed[...], channels + 1)
    for k in range(4):
        fill(q_side.at[0], k, side[k], channels + 2 + k)
    fill(static_side, wet_main, side[4], channels + 6)
    fill(static_side, bed_main, side[5], channels + 7)

    settle = [[settle_base * params[0, k] for k in range(fractions)]]
    inv_crit = [[1.0 / (critical_base * params[1, k]) for k in range(fractions)]]
    erode = [[erode_base * params[2, k] for k in range(fractions)]]

    def by_group(values):
        out = jnp.full((SUB, LANES), values[0], jnp.float32)
        for k in range(1, fractions):
            out = jnp.where(group == k, values[k], out)
        return out

    side_coeffs = ([by_group(settle[0])], [by_group(inv_crit[0])], [by_group(erode[0])])
    main_coeffs = (settle[0], inv_crit[0], erode[0])

    def turn(x, shift):
        shift = shift % LANES
        return pltpu.roll(x, shift, 1) if shift else x

    def start_of(k):
        return max(k - 3, 0) * width

    def low_edge(x, k):
        return turn(x, 1 - RIM - start_of(k))

    def high_edge(x, k):
        return turn(x, LANES - 1 - 3 * RIM - start_of(k))

    first_lane = lane == 0
    last_lane = lane == LANES - 1

    def rows_at(ref, p, row):
        return ref[p, pl.ds(row, SUB), :]

    def statics(block, carry):
        r0 = pl.multiple_of(top + block * SUB, SUB)
        for ref, is_main in ((static_side, False), (static_main, True)):
            w = rows_at(ref, wet_main, r0)
            b_plus = rows_at(ref, bed_main, r0 + 1)
            b_minus = rows_at(ref, bed_main, r0 - 1)
            b = rows_at(ref, bed_main, r0)
            w_right, b_right = pltpu.roll(w, LANES - 1, 1), pltpu.roll(b, LANES - 1, 1)
            b_left = pltpu.roll(b, 1, 1)
            if is_main:
                w_edge, b_edge = rows_at(static_side, wet_main, r0), rows_at(static_side, bed_main, r0)
                w_right = jnp.where(last_lane, high_edge(w_edge, 0), w_right)
                b_right = jnp.where(last_lane, high_edge(b_edge, 0), b_right)
                b_left = jnp.where(first_lane, low_edge(b_edge, 0), b_left)
            at = pl.ds(r0, SUB)
            ref[2, at, :] = 0.5 * (w * rows_at(ref, wet_main, r0 + 1))
            ref[3, at, :] = 0.5 * (w * w_right)
            ref[4, at, :] = (0.5 * gravity) * (b_plus - b_minus)
            ref[5, at, :] = (0.5 * gravity) * (b_right - b_left)
            ref[6, at, :] = time_step * w
        return carry

    lax.fori_loop(0, blocks, statics, 0)

    def slopes(block, level):
        r0 = pl.multiple_of(top + block * SUB, SUB)
        at = pl.ds(r0, SUB)
        for q, s, n in ((q_side, slope_side, 4), (q_main, slope_main, channels)):
            if n == 4 and level == SUBSTEPS - 1:
                continue
            q = q.at[level % 2]
            for k in range(n):
                s[k, at, :] = half_minmod(rows_at(q, k, r0 - 1), rows_at(q, k, r0), rows_at(q, k, r0 + 1))

    def row_fluxes(q, s, f, static, n, r0):
        lefts = [rows_at(q, k, r0) + rows_at(s, k, r0) for k in range(n)]
        rights = [rows_at(q, k, r0 + 1) - rows_at(s, k, r0 + 1) for k in range(n)]
        out = face_fluxes(lefts, rights, 1, rows_at(static, 2, r0))
        for k in range(n):
            f[k, pl.ds(r0, SUB), :] = out[k]
        return [rows_at(f, k, r0 - 1) - out[k] for k in range(n)]

    def col_fluxes(here, static, n, r0, edges):
        lefts, rights = [], []
        for k in range(n):
            before, after = pltpu.roll(here[k], 1, 1), pltpu.roll(here[k], LANES - 1, 1)
            if edges is not None:
                before = jnp.where(first_lane, low_edge(edges[min(k, 3)], k), before)
                after = jnp.where(last_lane, high_edge(edges[min(k, 3)], k), after)
            s = half_minmod(before, here[k], after)
            lefts.append(here[k] + s)
            rights.append(pltpu.roll(here[k] - s, LANES - 1, 1))
        return face_fluxes(lefts, rights, 2, rows_at(static, 3, r0))

    def update(here, net, static, coeffs, r0):
        step = rows_at(static, 6, r0)
        inv = pl.reciprocal(jnp.maximum(here[0], depth_floor))
        u, v = here[1] * inv, here[2] * inv
        squared = u * u + v * v + 1e-06
        drag = drag_coeff * jnp.sqrt(squared)
        new = [
            here[0] + step * net[0],
            here[1] + step * (net[1] - here[0] * rows_at(static, 4, r0) - drag * u),
            here[2] + step * (net[2] - here[0] * rows_at(static, 5, r0) - drag * v),
        ]
        changes = []
        for k in range(len(here) - 3):
            m = here[3 + k]
            settled = coeffs[0][k] * m * inv
            eroded = coeffs[2][k] * jnp.maximum(squared * coeffs[1][k] - 1.0, 0.0)
            change = step * (settled - eroded)
            changes.append(change)
            new.append(m + step * net[3 + k] - change)
        return new, changes

    def advance(block, level, rows_only=False):
        r0 = pl.multiple_of(top + block * SUB, SUB)
        at = pl.ds(r0, SUB)
        last = level == SUBSTEPS - 1
        qs, qm = q_side.at[level % 2], q_main.at[level % 2]
        slopes(block + 1, level)
        if rows_only:
            row_fluxes(qm, slope_main, flux_main, static_main, channels, r0)
            return
        edges = [rows_at(qs, k, r0) for k in range(4)]
        side_flux = col_fluxes(edges, static_side, 4, r0, None)
        if not last:
            net = row_fluxes(qs, slope_side, flux_side, static_side, 4, r0)
            net = [x + (pltpu.roll(f, 1, 1) - f) for x, f in zip(net, side_flux)]
            new, _ = update(edges, net, static_side, side_coeffs, r0)
            for k in range(4):
                q_side[(level + 1) % 2, k, at, :] = new[k]
        net = row_fluxes(qm, slope_main, flux_main, static_main, channels, r0)
        here = [rows_at(qm, k, r0) for k in range(channels)]
        fluxes = col_fluxes(here, static_main, channels, r0, edges)
        for k in range(channels):
            edge = side_flux[min(k, 3)]
            f = jnp.where(last_lane, turn(edge, LANES - 3 * RIM - start_of(k)), fluxes[k])
            net[k] = net[k] + (jnp.where(first_lane, low_edge(edge, k), pltpu.roll(fluxes[k], 1, 1)) - f)
        new, changes = update(here, net, static_main, main_coeffs, r0)
        if last:
            out = pl.ds(pl.multiple_of(r0 - body, SUB), SUB)
            depth_out[out, :] = new[0]
            flow_out[0, out, :] = new[1]
            flow_out[1, out, :] = new[2]
            for k in range(fractions):
                mud_out[k, out, :] = new[3 + k]
        else:
            for k in range(channels):
                q_main[(level + 1) % 2, k, at, :] = new[k]
        for k in range(fractions):
            if level == 0:
                exchanged[k, at, :] = changes[k]
            else:
                exchanged[k, at, :] = exchanged[k, at, :] + changes[k]

    for level in range(SUBSTEPS):
        last = level == SUBSTEPS - 1

        def advance_step(block, carry, level=level):
            advance(block, level)
            return carry

        slopes(0, level)
        if last:
            advance(0, level, rows_only=True)
            lax.fori_loop(1, blocks - 1, advance_step, 0, unroll=UNROLL)
        else:
            lax.fori_loop(0, blocks, advance_step, 0, unroll=UNROLL)

    coarse_rows = rows // 4
    code_ref[...] = code[...]
    parts = [[exchanged[f, pl.ds(body + k, coarse_rows, stride=4), :] for k in range(4)] for f in range(fractions)]
    codes = [code_ref[pl.ds(k, coarse_rows, stride=4), :] for k in range(4)]
    to_coarse = (
        lax.broadcasted_iota(jnp.int32, (LANES, LANES), 0) // 4 == lax.broadcasted_iota(jnp.int32, (LANES, LANES), 1)
    ).astype(jnp.bfloat16)
    coarse_start, frame_start = starts_of(lax.axis_index("col"), band_cols)
    total = None
    for col_shift in range(7):
        sums = [None] * fractions
        for row_shift in range(3):
            hits = [c == row_shift * 7 + col_shift for c in codes]
            for f in range(fractions):
                part = None
                for k in range(4):
                    x = jnp.where(hits[k], parts[f][k], 0.0)
                    part = x if part is None else part + x
                if row_shift != 1:
                    part = pltpu.roll(part, 1 if row_shift == 2 else coarse_rows - 1, 0)
                sums[f] = part if sums[f] is None else sums[f] + part
        rest = jnp.concatenate(sums, axis=0)
        z = None
        for _ in range(3):
            term = rest.astype(jnp.bfloat16)
            rest = rest - term.astype(jnp.float32)
            moved = jnp.dot(term, to_coarse, preferred_element_type=jnp.float32)
            z = moved if z is None else z + moved
        z = pltpu.roll(z, (coarse_start - frame_start + col_shift - 3 + LANES) % LANES, 1)
        total = z if total is None else total + z
    partial[...] = total


def bed_kernel(geometry, sums, bed, cells, bed_out, deposit_out, fine, frame_ref, total_ref):
    band_cols, cols_count, strip_rows = geometry
    rows = cells.shape[0]
    band_rows = rows // 4
    fractions = sums.shape[1] // band_rows
    total = sums[0]
    for d in range(1, cols_count):
        total = total + sums[d]
    total_ref[...] = (exner_factor / 16.0) * total
    at = lax.axis_index("col") * strip_rows
    frame_ref[...] = jnp.zeros_like(frame_ref)
    whole = None
    for f in range(fractions):
        part = total_ref[pl.ds(f * band_rows, band_rows), :]
        whole = part if whole is None else whole + part
        deposit_out[f, :, :] = total_ref[pl.ds(f * band_rows + at, strip_rows), :]
    frame_ref[pl.ds(SUB, band_rows), :] = bed[pl.ds(SUB, band_rows), :] + whole
    bed_out[...] = frame_ref[pl.ds(SUB + at, strip_rows), :]
    for block in range(rows // SUB):
        here = pl.ds(block * SUB, SUB)
        cell_row, cell_col = split_cells(cells[here, :].astype(jnp.float32), band_cols)
        fine[here, :] = lookup(frame_ref, block, row_shift_of(cell_row, block), cell_col)


def local(water_depth, discharge, sediment, bed_level, cell_map, wet_mask, sediment_params):
    tile_rows, tile_cols = water_depth.shape
    fractions = sediment.shape[0]
    strip_rows, band_cols = bed_level.shape
    cols_count = lax.axis_size("col")
    rows_count = lax.axis_size("row")
    band_rows = tile_rows // 4
    f32 = functools.partial(jax.ShapeDtypeStruct, dtype=jnp.float32)
    narrow = band_cols == LANES
    col_at = lax.axis_index("col")
    frame_start = starts_of(col_at, band_cols)[1]
    chunks = band_cols // LANES
    extra = (5 + fractions - LANES // (2 * RIM)) * folded_rows(tile_rows) * SUB
    pack_rows = tile_rows + extra + -(-chunks * strip_rows // SUB) * SUB

    packed = pl.pallas_call(
        pack_kernel, out_shape=f32((pack_rows, LANES)), in_specs=[vmem()] * 6, out_specs=vmem(),
        compiler_params=params_of(),
    )(water_depth, discharge, sediment, wet_mask, cell_map, bed_level)
    packs = lax.all_gather(packed, "col", axis=0)

    frames = []
    if not narrow:
        strips = packs[:, tile_rows + extra : tile_rows + extra + chunks * strip_rows]
        band = strips.reshape(cols_count, chunks, strip_rows, LANES).transpose(0, 2, 1, 3).reshape(band_rows, band_cols)
        wide = jnp.pad(band, ((0, 0), (LANES, LANES)))
        frames = [lax.dynamic_slice(wide, (jnp.int32(0), frame_start + LANES), (band_rows, LANES))]
    edge_planes = 3 + fractions + 2 + 6
    side, bed, code, send_a, send_b, framed = pl.pallas_call(
        functools.partial(mid_kernel, (band_cols, cols_count, strip_rows, narrow)),
        out_shape=(
            f32((6, tile_rows, LANES)), f32((tile_rows, LANES)), jax.ShapeDtypeStruct((tile_rows, LANES), jnp.int32),
            f32((edge_planes, SUB, LANES)), f32((edge_planes, SUB, LANES)), f32((band_rows + 2 * SUB, LANES)),
        ),
        in_specs=[vmem()] * (6 + len(frames)), out_specs=(vmem(),) * 6, compiler_params=params_of(),
    )(water_depth, discharge, sediment, wet_mask, cell_map, packs, *frames)

    pairs_a = [p for i in range(0, rows_count - 1, 2) for p in ((i, i + 1), (i + 1, i))]
    pairs_b = [p for i in range(1, rows_count - 1, 2) for p in ((i, i + 1), (i + 1, i))]
    recv_a = lax.ppermute(send_a, "row", pairs_a)
    recv_b = lax.ppermute(send_b, "row", pairs_b)

    channels = 3 + fractions
    span = tile_rows + 2 * RIM + 3 * SUB
    space = functools.partial(pltpu.VMEM, dtype=jnp.float32)
    depth_out, discharge_out, sediment_out, partial = pl.pallas_call(
        functools.partial(flow_kernel, band_cols),
        out_shape=(
            f32(water_depth.shape), f32(discharge.shape), f32(sediment.shape), f32((fractions * band_rows, LANES)),
        ),
        in_specs=[vmem()] * 7 + [smem()] + [vmem()] * 2, out_specs=(vmem(),) * 4, compiler_params=params_of(),
        scratch_shapes=[
            space((2, channels, span, LANES)), space((2, 4, span, LANES)), space((7, span, LANES)),
            space((7, span, LANES)), space((channels, span, LANES)), space((4, span, LANES)),
            space((channels, span, LANES)), space((4, span, LANES)), space((fractions, span, LANES)),
            pltpu.VMEM((tile_rows, LANES), jnp.int32),
        ],
    )(water_depth, discharge, sediment, wet_mask, bed, side, code, sediment_params, recv_a, recv_b)

    sums = lax.all_gather(partial, "col", axis=0)
    geometry = (band_cols if narrow else LANES, cols_count, strip_rows)
    if narrow:
        look_cells = cell_map
    else:
        wide = jnp.zeros((fractions, band_rows, band_cols + 2 * LANES), jnp.float32)
        for d in range(cols_count):
            start = LANES + d * (tile_cols // 4) - (LANES - tile_cols // 4) // 2
            wide = wide.at[:, :, start : start + LANES].add(sums[d].reshape(fractions, band_rows, LANES))
        share = lax.dynamic_slice_in_dim(wide, col_at * strip_rows, strip_rows, axis=1)[:, :, LANES:-LANES]
        deposit_wide = exner_factor / 16.0 * share
        bed_wide = bed_level + jnp.sum(deposit_wide, axis=0)
        sums = lax.dynamic_slice_in_dim(wide, frame_start + LANES, LANES, axis=2).reshape(1, -1, LANES)
        geometry = (LANES, 1, strip_rows)
        look_cells = cell_map // band_cols * LANES + cell_map % band_cols - frame_start
    bed_new, deposit, fine_bed = pl.pallas_call(
        functools.partial(bed_kernel, geometry),
        out_shape=(f32((strip_rows, LANES)), f32((fractions, strip_rows, LANES)), f32((tile_rows, LANES))),
        in_specs=[vmem()] * 3, out_specs=(vmem(),) * 3, compiler_params=params_of(),
        scratch_shapes=[space((band_rows + 2 * SUB, LANES)), space((fractions * band_rows, LANES))],
    )(sums, framed, look_cells)
    if not narrow:
        bed_new, deposit = bed_wide, deposit_wide
    return (depth_out, discharge_out, sediment_out, fine_bed, bed_new, deposit)


def solution(mesh):
    placed = (
        P("row", "col"),
        P(None, "row", "col"),
        P(None, "row", "col"),
        P(("row", "col"), None),
        P("row", "col"),
        P("row", "col"),
        P(),
    )
    return jax.shard_map(
        local,
        mesh=mesh,
        in_specs=placed,
        out_specs=(
            P("row", "col"),
            P(None, "row", "col"),
            P(None, "row", "col"),
            P("row", "col"),
            P(("row", "col"), None),
            P(None, ("row", "col"), None),
        ),
        check_vma=False,
    )
```

```python
import functools

import jax
import jax.numpy as jnp
from jax import lax
from jax.experimental import pallas as pl
from jax.experimental.pallas import tpu as pltpu
from jax.sharding import PartitionSpec as P

SUBSTEPS = 4
LANES = 128
SUB = 8
UNROLL = 2
AHEAD = 1
TOP = SUB
RIM = 2 * SUBSTEPS

gravity = 1.0
time_step = 0.2
depth_floor = 1.25
drag_coeff = 0.02
settle_base = 0.05
critical_base = 0.05
erode_base = 0.002
exner_factor = 400.0


def vmem():
    return pl.BlockSpec(memory_space=pltpu.VMEM)


def smem():
    return pl.BlockSpec(memory_space=pltpu.SMEM)


def lane_ids(shape):
    return lax.broadcasted_iota(jnp.int32, shape, len(shape) - 1)


def params_of(limit=16 << 20):
    return pltpu.CompilerParams(vmem_limit_bytes=limit)


def pick(table, index):
    return jnp.take_along_axis(table, index, axis=1, mode="promise_in_bounds")


def hbm():
    return pl.BlockSpec(memory_space=pltpu.HBM)


def turn(x, shift):
    shift = shift % LANES
    return pltpu.roll(x, shift, 1) if shift else x


def folded_rows(rows):
    return -(-rows // SUB // (LANES // (2 * RIM)))


def pack_kernel(depth, flow, mud, wet, cells, strip, params, planes, coeffs, out, wet_ref, cell_ref, strip_ref, param_ref, sems):
    rows = depth.shape[0]
    fractions = mud.shape[0]
    moves = [
        (depth, planes.at[0]), (flow, planes.at[pl.ds(1, 2)]), (mud, planes.at[pl.ds(3, fractions)]), (wet, wet_ref),
        (cells, cell_ref), (strip, strip_ref), (params, param_ref),
    ]
    copies = [pltpu.make_async_copy(src, dst, sems.at[k]) for k, (src, dst) in enumerate(moves)]
    for copy in copies:
        copy.start()
    for copy in copies:
        copy.wait()
    count = 5 + fractions
    lane = lane_ids((SUB, LANES))
    group = lane // RIM
    pairs = LANES // (2 * RIM)
    spare = [[None] * folded_rows(rows) for _ in range(pairs, count)]
    for block in range(rows // SUB):
        at = pl.ds(block * SUB, SUB)
        planes[count - 2, at, :] = wet_ref[at, :].astype(jnp.float32)
        planes[count - 1, at, :] = cell_ref[at, :].astype(jnp.float32)
        packed = None
        for p in range(count):
            x = planes[p, at, :]
            slot = p if p < pairs else block % pairs
            low, high = turn(x, 2 * RIM * slot), turn(x, 2 * RIM * slot + 2 * RIM)
            old = packed if p < pairs else spare[p - pairs][block // pairs]
            both = jnp.where(group == 2 * slot, low, high)
            new = both if old is None else jnp.where(group // 2 == slot, both, old)
            if p < pairs:
                packed = new
            else:
                spare[p - pairs][block // pairs] = new
        out[at, :] = packed
    start = rows
    for x in [x for p in spare for x in p]:
        out[pl.ds(start, SUB), :] = x
        start += SUB
    strip_rows = strip.shape[0]
    for chunk in range(strip.shape[1] // LANES):
        out[pl.ds(start + chunk * strip_rows, strip_rows), :] = strip_ref[:, chunk * LANES : (chunk + 1) * LANES]
    for c in range(3):
        each = []
        for k in range(fractions):
            value = jnp.full((SUB, LANES), param_ref[c, k], jnp.float32)
            value = (settle_base * value, 1.0 / (critical_base * value), erode_base * value)[c]
            coeffs[c, k, :, :] = value
            each.append(value)
        mixed = each[0]
        for k in range(1, fractions):
            mixed = jnp.where(lane // (4 * RIM) == k, each[k], mixed)
        coeffs[c, fractions, :, :] = mixed


def spread_rows(frame_ref, block, shift):
    first = SUB + block * (SUB // 4) + shift
    low = jnp.broadcast_to(frame_ref[pl.ds(first, 1), :], (SUB, LANES))
    high = jnp.broadcast_to(frame_ref[pl.ds(first + 1, 1), :], (SUB, LANES))
    sub = lax.broadcasted_iota(jnp.int32, (SUB, LANES), 0)
    return jnp.where(sub < 4, low, high)


def split_cells(cells, band_cols):
    row = jnp.floor((cells + 0.5) * (1.0 / band_cols))
    return row.astype(jnp.int32), (cells - row * band_cols).astype(jnp.int32)


def row_shift_of(cell_row, block):
    sub = lax.broadcasted_iota(jnp.int32, (SUB, LANES), 0)
    return cell_row - (block * (SUB // 4) + sub // 4)


def lookup(frame_ref, block, shift, column):
    found = pick(spread_rows(frame_ref, block, 0), column)
    below = pick(spread_rows(frame_ref, block, -1), column)
    above = pick(spread_rows(frame_ref, block, 1), column)
    return jnp.where(shift == 0, found, jnp.where(shift < 0, below, above))


def starts_of(col_at, band_cols):
    coarse_start = col_at * (LANES // 4)
    return coarse_start, 0 if band_cols == LANES else coarse_start - (LANES - LANES // 4) // 2


def fill_frame(frame_ref, rows_of):
    frame_ref[...] = jnp.zeros_like(frame_ref)
    for r0, value in rows_of:
        frame_ref[pl.ds(SUB + r0, value.shape[0]), :] = value


def side_maker(geometry, planes, packs, frame_ref):
    band_cols, cols_count = geometry[:2]
    count, rows = planes.shape[:2]
    fractions = count - 5
    col_at = lax.axis_index("col")
    coarse_start, frame_start = starts_of(col_at, band_cols)
    wet_at, cell_at = count - 2, count - 1
    pairs = LANES // (2 * RIM)
    lane = lane_ids((SUB, LANES))
    width = 4 * RIM
    inside = lane % width
    group = lane // width
    is_low = inside < RIM
    is_high = inside >= 3 * RIM
    is_first = inside < 2 * RIM
    has_low = jnp.where(col_at > 0, 1.0, 0.0)
    has_high = jnp.where(col_at < cols_count - 1, 1.0, 0.0)
    scale = jnp.where(is_low, has_low, jnp.where(is_high, has_high, 1.0))
    left = jnp.maximum(col_at - 1, 0)
    right = jnp.minimum(col_at + 1, cols_count - 1)

    def make(block):
        at = pl.ds(block * SUB, SUB)

        def gather_to(p, base):
            if p < pairs:
                source, slot = at, p
            else:
                source = pl.ds(rows + ((p - pairs) * folded_rows(rows) + block // pairs) * SUB, SUB)
                slot = block % pairs
            x = planes[p, at, :]
            low = turn(packs[left, source, :], base - 2 * RIM * slot - RIM)
            high = turn(packs[right, source, :], base + 3 * RIM - 2 * RIM * slot)
            own = jnp.where(is_first, turn(x, base + RIM), turn(x, base + 3 * RIM))
            return jnp.where(is_low, low, jnp.where(is_high, high, own))

        def for_all(p):
            x = gather_to(p, 0)
            x = jnp.where(lane < width, x, pltpu.roll(x, width, 1))
            return jnp.where(lane < 2 * width, x, pltpu.roll(x, 2 * width, 1)) * scale

        sides = [for_all(p) for p in range(3)]
        each = gather_to(3, 0)
        for k in range(1, fractions):
            each = jnp.where(group == k, gather_to(3 + k, k * width), each)
        sides.append(each * scale)
        sides.append(for_all(wet_at))
        side_row, side_col = split_cells(for_all(cell_at), band_cols)
        side_at = jnp.where(scale > 0.0, side_col - frame_start, 0)
        sides.append(lookup(frame_ref, block, row_shift_of(side_row, block), side_at) * scale)
        cell_row, cell_col = split_cells(planes[cell_at, at, :], band_cols)
        shift = row_shift_of(cell_row, block)
        bed = lookup(frame_ref, block, shift, cell_col - frame_start)
        return sides, bed, (shift + 1) * 7 + (cell_col - coarse_start - lane // 4 + 3)

    return make


def edge_kernel(geometry, planes, packs, *refs):
    _, cols_count, strip_rows, from_packs = geometry
    frame = None if from_packs else refs[0]
    send_a, send_b, code, frame_ref = refs[0 if from_packs else 1 :]
    count, rows = planes.shape[:2]
    pairs = LANES // (2 * RIM)
    strip_at = rows + (count - pairs) * folded_rows(rows) * SUB
    if from_packs:
        fill_frame(
            frame_ref, [(d * strip_rows, packs[d, pl.ds(strip_at, strip_rows), :]) for d in range(cols_count)]
        )
    else:
        fill_frame(frame_ref, [(0, frame[...])])
    make = side_maker(geometry, planes, packs, frame_ref)
    parity = lax.axis_index("row") % 2
    last = rows // SUB - 1
    done = [make(0), make(last)]
    for out, turned in ((send_a, parity == 1), (send_b, parity == 0)):
        for p in range(count + 6):
            first, final = [
                planes[p, pl.ds(b * SUB, SUB), :] if p < count - 1 else bed if p == count - 1 else sides[p - count]
                for b, (sides, bed, _) in zip((0, last), done)
            ]
            out[p, :, :] = jnp.where(turned, first, final)
    code[0, :, :] = done[0][2]
    code[1, :, :] = done[1][2]


def half_minmod(before, here, after):
    low = 0.5 * (here - before)
    high = 0.5 * (after - here)
    return jnp.maximum(jnp.minimum(low, high), jnp.minimum(jnp.maximum(low, high), 0.0))


def face_fluxes(lefts, rights, normal, half_open):
    speed_l = lefts[normal] * pl.reciprocal(jnp.maximum(lefts[0], depth_floor))
    speed_r = rights[normal] * pl.reciprocal(jnp.maximum(rights[0], depth_floor))
    wave = jnp.maximum(
        jnp.abs(speed_l) + jnp.sqrt(gravity * lefts[0]), jnp.abs(speed_r) + jnp.sqrt(gravity * rights[0])
    )
    to_l = half_open * (speed_l + wave)
    to_r = half_open * (speed_r - wave)
    out = [l * to_l + r * to_r for l, r in zip(lefts, rights)]
    out[normal] = out[normal] + (0.5 * gravity) * half_open * (lefts[0] * lefts[0] + rights[0] * rights[0])
    return out


def stepper(coeffs, q_main, q_side, static_main, static_side, slope_main, slope_side, flux_main, flux_side, exchanged):
    channels = q_main.shape[1]
    fractions = channels - 3
    lane = lane_ids((SUB, LANES))
    width = 4 * RIM
    first_lane = lane == 0
    last_lane = lane == LANES - 1
    wet_at, bed_at = 0, 1

    def coeffs_of(k):
        return [coeffs[c, k, :, :] for c in range(3)]

    def start_of(k):
        return max(k - 3, 0) * width

    def low_edge(x, k):
        return turn(x, 1 - RIM - start_of(k))

    def high_edge(x, k):
        return turn(x, LANES - 1 - 3 * RIM - start_of(k))

    def rows_at(ref, p, row):
        return ref[p, pl.ds(row, SUB), :]

    def statics(block):
        r0 = TOP + block * SUB
        for ref, is_main in ((static_side, False), (static_main, True)):
            w = rows_at(ref, wet_at, r0)
            b_plus = rows_at(ref, bed_at, r0 + 1)
            b_minus = rows_at(ref, bed_at, r0 - 1)
            b = rows_at(ref, bed_at, r0)
            w_right, b_right = pltpu.roll(w, LANES - 1, 1), pltpu.roll(b, LANES - 1, 1)
            b_left = pltpu.roll(b, 1, 1)
            if is_main:
                w_edge, b_edge = rows_at(static_side, wet_at, r0), rows_at(static_side, bed_at, r0)
                w_right = jnp.where(last_lane, high_edge(w_edge, 0), w_right)
                b_right = jnp.where(last_lane, high_edge(b_edge, 0), b_right)
                b_left = jnp.where(first_lane, low_edge(b_edge, 0), b_left)
            at = pl.ds(r0, SUB)
            ref[2, at, :] = 0.5 * (w * rows_at(ref, wet_at, r0 + 1))
            ref[3, at, :] = 0.5 * (w * w_right)
            ref[4, at, :] = (0.5 * gravity) * (b_plus - b_minus)
            ref[5, at, :] = (0.5 * gravity) * (b_right - b_left)
            ref[6, at, :] = time_step * w

    def slopes(block, level):
        r0 = pl.multiple_of(TOP + block * SUB, SUB)
        at = pl.ds(r0, SUB)
        for q, s, n in ((q_side, slope_side, 4), (q_main, slope_main, channels)):
            if n == 4 and level == SUBSTEPS - 1:
                continue
            q = q.at[level % 2]
            for k in range(n):
                s[k, at, :] = half_minmod(rows_at(q, k, r0 - 1), rows_at(q, k, r0), rows_at(q, k, r0 + 1))

    def row_fluxes(q, s, f, static, n, r0):
        lefts = [rows_at(q, k, r0) + rows_at(s, k, r0) for k in range(n)]
        rights = [rows_at(q, k, r0 + 1) - rows_at(s, k, r0 + 1) for k in range(n)]
        out = face_fluxes(lefts, rights, 1, rows_at(static, 2, r0))
        for k in range(n):
            f[k, pl.ds(r0, SUB), :] = out[k]
        return [rows_at(f, k, r0 - 1) - out[k] for k in range(n)]

    def col_fluxes(here, static, n, r0, edges):
        lefts, rights = [], []
        for k in range(n):
            before, after = pltpu.roll(here[k], 1, 1), pltpu.roll(here[k], LANES - 1, 1)
            if edges is not None:
                before = jnp.where(first_lane, low_edge(edges[min(k, 3)], k), before)
                after = jnp.where(last_lane, high_edge(edges[min(k, 3)], k), after)
            s = half_minmod(before, here[k], after)
            lefts.append(here[k] + s)
            rights.append(pltpu.roll(here[k] - s, LANES - 1, 1))
        return face_fluxes(lefts, rights, 2, rows_at(static, 3, r0))

    def update(here, net, static, coeffs, r0):
        step = rows_at(static, 6, r0)
        inv = pl.reciprocal(jnp.maximum(here[0], depth_floor))
        u, v = here[1] * inv, here[2] * inv
        squared = u * u + v * v + 1e-06
        drag = drag_coeff * jnp.sqrt(squared)
        new = [
            here[0] + step * net[0],
            here[1] + step * (net[1] - here[0] * rows_at(static, 4, r0) - drag * u),
            here[2] + step * (net[2] - here[0] * rows_at(static, 5, r0) - drag * v),
        ]
        changes = []
        for k in range(len(here) - 3):
            m = here[3 + k]
            settle, inv_critical, erode = coeffs[k]
            change = step * (settle * m * inv - erode * jnp.maximum(squared * inv_critical - 1.0, 0.0))
            changes.append(change)
            new.append(m + step * net[3 + k] - change)
        return new, changes

    def advance(block, level, rows_only=False):
        r0 = pl.multiple_of(TOP + block * SUB, SUB)
        at = pl.ds(r0, SUB)
        last = level == SUBSTEPS - 1
        qs, qm = q_side.at[level % 2], q_main.at[level % 2]
        slopes(block + 1, level)
        if rows_only:
            row_fluxes(qm, slope_main, flux_main, static_main, channels, r0)
            if not last:
                row_fluxes(qs, slope_side, flux_side, static_side, 4, r0)
            return
        edges = [rows_at(qs, k, r0) for k in range(4)]
        side_flux = col_fluxes(edges, static_side, 4, r0, None)
        if not last:
            net = row_fluxes(qs, slope_side, flux_side, static_side, 4, r0)
            net = [x + (pltpu.roll(f, 1, 1) - f) for x, f in zip(net, side_flux)]
            new, _ = update(edges, net, static_side, [coeffs_of(fractions)], r0)
            for k in range(4):
                q_side[(level + 1) % 2, k, at, :] = new[k]
        net = row_fluxes(qm, slope_main, flux_main, static_main, channels, r0)
        here = [rows_at(qm, k, r0) for k in range(channels)]
        fluxes = col_fluxes(here, static_main, channels, r0, edges)
        for k in range(channels):
            edge = side_flux[min(k, 3)]
            f = jnp.where(last_lane, turn(edge, LANES - 3 * RIM - start_of(k)), fluxes[k])
            net[k] = net[k] + (jnp.where(first_lane, low_edge(edge, k), pltpu.roll(fluxes[k], 1, 1)) - f)
        new, changes = update(here, net, static_main, [coeffs_of(k) for k in range(fractions)], r0)
        for k in range(channels):
            q_main[(level + 1) % 2, k, at, :] = new[k]
        for k in range(fractions):
            if level == 0:
                exchanged[k, at, :] = changes[k]
            else:
                exchanged[k, at, :] = exchanged[k, at, :] + changes[k]

    def sweep(first, end, level, unroll=None):
        def one(block, carry):
            advance(block, level)
            return carry

        if unroll is None:
            for block in range(first, end):
                advance(block, level)
        else:
            lax.fori_loop(first, end, one, 0, unroll=unroll)

    return statics, slopes, advance, sweep


def early_kernel(
    geometry, planes, packs, frame_ref, send_a, send_b, ends, coeffs,
    q_main, q_side, static_main, static_side, flux_main, flux_side, exchanged, code, slope_main, slope_side,
):
    count, rows = planes.shape[:2]
    channels = count - 2
    body = TOP + RIM
    parity = lax.axis_index("row") % 2
    blocks = rows // SUB
    for k in range(channels):
        q_main[0, k, pl.ds(body, rows), :] = planes[k]
    static_main[0, pl.ds(body, rows), :] = planes[channels]
    for block, is_first in ((0, True), (blocks - 1, False)):
        at = pl.ds(body + block * SUB, SUB)
        mine = [
            jnp.where((parity == 1) == is_first, send_a[p], send_b[p]) for p in range(channels + 1, channels + 8)
        ]
        static_main[1, at, :] = mine[0]
        for k in range(4):
            q_side[0, k, at, :] = mine[1 + k]
        static_side[0, at, :] = mine[5]
        static_side[1, at, :] = mine[6]
        code[pl.ds(block * SUB, SUB), :] = ends[0 if is_first else 1]
    make = side_maker(geometry, planes, packs, frame_ref)
    for block in range(1, blocks - 1):
        at = pl.ds(body + block * SUB, SUB)
        sides, bed, coded = make(block)
        static_main[1, at, :] = bed
        for k in range(4):
            q_side[0, k, at, :] = sides[k]
        static_side[0, at, :] = sides[4]
        static_side[1, at, :] = sides[5]
        code[pl.ds(block * SUB, SUB), :] = coded
    statics, slopes, advance, sweep = stepper(
        coeffs, q_main, q_side, static_main, static_side, slope_main, slope_side, flux_main, flux_side, exchanged
    )
    total = blocks + 2
    for block in range(1, total - 2):
        statics(block)
    for level in range(AHEAD):
        slopes(1 + level, level)
        advance(1 + level, level, rows_only=True)
        sweep(2 + level, total - 2 - level, level, UNROLL)


def late_kernel(
    band_cols, recv_a, recv_b, coeffs, code,
    q_main_in, q_side_in, static_main_in, static_side_in, flux_main_in, flux_side_in, exchanged_in,
    depth_out, flow_out, mud_out, partial,
    q_main, q_side, static_main, static_side, flux_main, flux_side, exchanged,
    slope_main, slope_side, sems,
):
    del q_main_in, q_side_in, static_main_in, static_side_in, flux_main_in, flux_side_in, exchanged_in
    rows = code.shape[0]
    channels = q_main.shape[1]
    fractions = channels - 3
    body = TOP + RIM
    parity = lax.axis_index("row") % 2
    total = rows // SUB + 2

    def fill(put, p):
        a, b = recv_a[p], recv_b[p]
        put(pl.ds(TOP, RIM), jnp.where(parity == 1, a, b))
        put(pl.ds(body + rows, RIM), jnp.where(parity == 1, b, a))

    for k in range(channels + 8):
        def put(at, x, k=k):
            if k < channels:
                q_main[0, k, at, :] = x
            elif k < channels + 2:
                static_main[k - channels, at, :] = x
            elif k < channels + 6:
                q_side[0, k - channels - 2, at, :] = x
            else:
                static_side[k - channels - 6, at, :] = x

        fill(put, k)
    statics, slopes, advance, sweep = stepper(
        coeffs, q_main, q_side, static_main, static_side, slope_main, slope_side, flux_main, flux_side, exchanged
    )
    for block in (0, total - 2, total - 1):
        statics(block)
    if total > 3:
        statics(1)
    for level in range(SUBSTEPS):
        slopes(0, level)
        if level < AHEAD:
            sweep(0, 2 + level, level)
            slopes(total - 2 - level, level)
            sweep(total - 2 - level, total, level)
        elif level < SUBSTEPS - 1:
            sweep(0, total, level, UNROLL)
        else:
            advance(0, level, rows_only=True)
            sweep(1, total - 1, level, UNROLL)
    final = q_main.at[SUBSTEPS % 2]
    here = pl.ds(body, rows)
    copies = [pltpu.make_async_copy(final.at[0, here], depth_out, sems.at[0])]
    copies.append(pltpu.make_async_copy(final.at[pl.ds(1, 2), here], flow_out, sems.at[1]))
    copies.append(pltpu.make_async_copy(final.at[pl.ds(3, fractions), here], mud_out, sems.at[2]))
    for copy in copies:
        copy.start()

    coarse_rows = rows // 4
    parts = [[exchanged[f, pl.ds(body + k, coarse_rows, stride=4), :] for k in range(4)] for f in range(fractions)]
    codes = [code[pl.ds(k, coarse_rows, stride=4), :] for k in range(4)]
    to_coarse = (
        lax.broadcasted_iota(jnp.int32, (LANES, LANES), 0) // 4 == lax.broadcasted_iota(jnp.int32, (LANES, LANES), 1)
    ).astype(jnp.bfloat16)
    coarse_start, frame_start = starts_of(lax.axis_index("col"), band_cols)
    moved_total = None
    for col_shift in range(7):
        sums = [None] * fractions
        for row_shift in range(3):
            hits = [c == row_shift * 7 + col_shift for c in codes]
            for f in range(fractions):
                part = None
                for k in range(4):
                    x = jnp.where(hits[k], parts[f][k], 0.0)
                    part = x if part is None else part + x
                if row_shift != 1:
                    part = pltpu.roll(part, 1 if row_shift == 2 else coarse_rows - 1, 0)
                sums[f] = part if sums[f] is None else sums[f] + part
        rest = jnp.concatenate(sums, axis=0)
        z = None
        for _ in range(3):
            term = rest.astype(jnp.bfloat16)
            rest = rest - term.astype(jnp.float32)
            moved = jnp.dot(term, to_coarse, preferred_element_type=jnp.float32)
            z = moved if z is None else z + moved
        z = pltpu.roll(z, (coarse_start - frame_start + col_shift - 3 + LANES) % LANES, 1)
        moved_total = z if moved_total is None else moved_total + z
    partial[...] = moved_total
    for copy in copies:
        copy.wait()


def bed_kernel(geometry, sums, bed, planes, bed_out, deposit_out, fine, frame_ref, total_ref):
    band_cols, cols_count, strip_rows = geometry
    cells = planes.at[planes.shape[0] - 1]
    rows = cells.shape[0]
    band_rows = rows // 4
    fractions = sums.shape[1] // band_rows
    total = sums[0]
    for d in range(1, cols_count):
        total = total + sums[d]
    total_ref[...] = (exner_factor / 16.0) * total
    at = lax.axis_index("col") * strip_rows
    frame_ref[...] = jnp.zeros_like(frame_ref)
    whole = None
    for f in range(fractions):
        part = total_ref[pl.ds(f * band_rows, band_rows), :]
        whole = part if whole is None else whole + part
        deposit_out[f, :, :] = total_ref[pl.ds(f * band_rows + at, strip_rows), :]
    frame_ref[pl.ds(SUB, band_rows), :] = bed[pl.ds(SUB, band_rows), :] + whole
    bed_out[...] = frame_ref[pl.ds(SUB + at, strip_rows), :]
    for block in range(rows // SUB):
        here = pl.ds(block * SUB, SUB)
        cell_row, cell_col = split_cells(cells[here, :], band_cols)
        fine[here, :] = lookup(frame_ref, block, row_shift_of(cell_row, block), cell_col)


def local(water_depth, discharge, sediment, bed_level, cell_map, wet_mask, sediment_params):
    tile_rows, tile_cols = water_depth.shape
    fractions = sediment.shape[0]
    strip_rows, band_cols = bed_level.shape
    cols_count = lax.axis_size("col")
    rows_count = lax.axis_size("row")
    band_rows = tile_rows // 4
    f32 = functools.partial(jax.ShapeDtypeStruct, dtype=jnp.float32)
    narrow = band_cols == LANES
    col_at = lax.axis_index("col")
    frame_start = starts_of(col_at, band_cols)[1]
    chunks = band_cols // LANES
    extra = (5 + fractions - LANES // (2 * RIM)) * folded_rows(tile_rows) * SUB
    pack_rows = tile_rows + extra + -(-chunks * strip_rows // SUB) * SUB

    channels = 3 + fractions
    count = channels + 2
    space = functools.partial(pltpu.VMEM, dtype=jnp.float32)
    arguments = (water_depth, discharge, sediment, wet_mask, cell_map, bed_level, sediment_params)
    planes, coeffs, packed = pl.pallas_call(
        pack_kernel,
        out_shape=(
            f32((count, tile_rows, LANES)), f32((3, fractions + 1, SUB, LANES)), f32((pack_rows, LANES)),
        ),
        in_specs=[hbm()] * 7, out_specs=(vmem(),) * 3, compiler_params=params_of(),
        scratch_shapes=[
            pltpu.VMEM((tile_rows, LANES), jnp.int32), pltpu.VMEM((tile_rows, LANES), jnp.int32),
            space(bed_level.shape), pltpu.SMEM(sediment_params.shape, jnp.float32), pltpu.SemaphoreType.DMA((7,)),
        ],
    )(*[pltpu.with_memory_space_constraint(x, pltpu.HBM) for x in arguments])
    packs = lax.all_gather(packed, "col", axis=0)

    frames = []
    if not narrow:
        strips = packs[:, tile_rows + extra : tile_rows + extra + chunks * strip_rows]
        band = strips.reshape(cols_count, chunks, strip_rows, LANES).transpose(0, 2, 1, 3).reshape(band_rows, band_cols)
        wide = jnp.pad(band, ((0, 0), (LANES, LANES)))
        frames = [lax.dynamic_slice(wide, (jnp.int32(0), frame_start + LANES), (band_rows, LANES))]
    geometry = (band_cols, cols_count, strip_rows, narrow)
    send_a, send_b, ends, framed = pl.pallas_call(
        functools.partial(edge_kernel, geometry),
        out_shape=(
            f32((count + 6, SUB, LANES)), f32((count + 6, SUB, LANES)),
            jax.ShapeDtypeStruct((2, SUB, LANES), jnp.int32), f32((band_rows + 2 * SUB, LANES)),
        ),
        in_specs=[vmem()] * (2 + len(frames)), out_specs=(vmem(),) * 4, compiler_params=params_of(),
    )(planes, packs, *frames)

    pairs_a = [p for i in range(0, rows_count - 1, 2) for p in ((i, i + 1), (i + 1, i))]
    pairs_b = [p for i in range(1, rows_count - 1, 2) for p in ((i, i + 1), (i + 1, i))]
    recv_a = lax.ppermute(send_a, "row", pairs_a)
    recv_b = lax.ppermute(send_b, "row", pairs_b)

    span = tile_rows + 2 * RIM + 3 * SUB
    state = (
        f32((2, channels, span, LANES)), f32((2, 4, span, LANES)), f32((7, span, LANES)), f32((7, span, LANES)),
        f32((channels, span, LANES)), f32((4, span, LANES)), f32((fractions, span, LANES)),
    )
    slope_space = [space((channels, span, LANES)), space((4, span, LANES))]
    *begun, code = pl.pallas_call(
        functools.partial(early_kernel, geometry),
        out_shape=(*state, jax.ShapeDtypeStruct((tile_rows, LANES), jnp.int32)),
        in_specs=[vmem()] * 7, out_specs=(vmem(),) * 8, compiler_params=params_of(), scratch_shapes=slope_space,
    )(planes, packs, framed, send_a, send_b, ends, coeffs)
    depth_out, discharge_out, sediment_out, partial = pl.pallas_call(
        functools.partial(late_kernel, band_cols),
        out_shape=(
            f32(water_depth.shape), f32(discharge.shape), f32(sediment.shape), f32((fractions * band_rows, LANES)),
            *state,
        ),
        in_specs=[vmem()] * 11, out_specs=(hbm(),) * 3 + (vmem(),) * 8, compiler_params=params_of(),
        input_output_aliases={4 + k: 4 + k for k in range(7)},
        scratch_shapes=[*slope_space, pltpu.SemaphoreType.DMA((3,))],
    )(recv_a, recv_b, coeffs, code, *begun)[:4]

    sums = lax.all_gather(partial, "col", axis=0)
    geometry = (band_cols if narrow else LANES, cols_count, strip_rows)
    if narrow:
        look_cells = planes
    else:
        wide = jnp.zeros((fractions, band_rows, band_cols + 2 * LANES), jnp.float32)
        for d in range(cols_count):
            start = LANES + d * (tile_cols // 4) - (LANES - tile_cols // 4) // 2
            wide = wide.at[:, :, start : start + LANES].add(sums[d].reshape(fractions, band_rows, LANES))
        share = lax.dynamic_slice_in_dim(wide, col_at * strip_rows, strip_rows, axis=1)[:, :, LANES:-LANES]
        deposit_wide = exner_factor / 16.0 * share
        bed_wide = bed_level + jnp.sum(deposit_wide, axis=0)
        sums = lax.dynamic_slice_in_dim(wide, frame_start + LANES, LANES, axis=2).reshape(1, -1, LANES)
        geometry = (LANES, 1, strip_rows)
        look_cells = (cell_map // band_cols * LANES + cell_map % band_cols - frame_start).astype(jnp.float32)[None]
    bed_new, deposit, fine_bed = pl.pallas_call(
        functools.partial(bed_kernel, geometry),
        out_shape=(f32((strip_rows, LANES)), f32((fractions, strip_rows, LANES)), f32((tile_rows, LANES))),
        in_specs=[vmem()] * 3, out_specs=(vmem(),) * 3, compiler_params=params_of(),
        scratch_shapes=[space((band_rows + 2 * SUB, LANES)), space((fractions * band_rows, LANES))],
    )(sums, framed, look_cells)
    if not narrow:
        bed_new, deposit = bed_wide, deposit_wide
    return (depth_out, discharge_out, sediment_out, fine_bed, bed_new, deposit)


def solution(mesh):
    placed = (
        P("row", "col"),
        P(None, "row", "col"),
        P(None, "row", "col"),
        P(("row", "col"), None),
        P("row", "col"),
        P("row", "col"),
        P(),
    )
    return jax.shard_map(
        local,
        mesh=mesh,
        in_specs=placed,
        out_specs=(
            P("row", "col"),
            P(None, "row", "col"),
            P(None, "row", "col"),
            P("row", "col"),
            P(("row", "col"), None),
            P(None, ("row", "col"), None),
        ),
        check_vma=False,
    )
```

```python
import functools

import jax
import jax.numpy as jnp
from jax import lax
from jax.experimental import pallas as pl
from jax.experimental.pallas import tpu as pltpu
from jax.sharding import PartitionSpec as P

SUBSTEPS = 4
LANES = 128
SUB = 8
GROUP = 1
STRAIGHT = 12
AHEAD = 1
TOP = SUB
SMALLEST = 1.1754944e-38
RIM = 2 * SUBSTEPS

gravity = 1.0
time_step = 0.2
depth_floor = 1.25
drag_coeff = 0.02
settle_base = 0.05
critical_base = 0.05
erode_base = 0.002
exner_factor = 400.0


def vmem():
    return pl.BlockSpec(memory_space=pltpu.VMEM)


def smem():
    return pl.BlockSpec(memory_space=pltpu.SMEM)


def lane_ids(shape):
    return lax.broadcasted_iota(jnp.int32, shape, len(shape) - 1)


def params_of(limit=16 << 20):
    return pltpu.CompilerParams(vmem_limit_bytes=limit)


def pick(table, index):
    return jnp.take_along_axis(table, index, axis=1, mode="promise_in_bounds")


def hbm():
    return pl.BlockSpec(memory_space=pltpu.HBM)


def turn(x, shift):
    shift = shift % LANES
    return pltpu.roll(x, shift, 1) if shift else x


def folded_rows(rows):
    return -(-rows // SUB // (LANES // (2 * RIM)))


def pack_kernel(depth, flow, mud, wet, cells, strip, params, planes, coeffs, out, wet_ref, cell_ref, strip_ref, param_ref, sems):
    rows = depth.shape[0]
    fractions = mud.shape[0]
    moves = [
        (depth, planes.at[0]), (flow, planes.at[pl.ds(1, 2)]), (mud, planes.at[pl.ds(3, fractions)]), (wet, wet_ref),
        (cells, cell_ref), (strip, strip_ref), (params, param_ref),
    ]
    copies = [pltpu.make_async_copy(src, dst, sems.at[k]) for k, (src, dst) in enumerate(moves)]
    for copy in copies:
        copy.start()
    for copy in copies:
        copy.wait()
    count = 5 + fractions
    lane = lane_ids((SUB, LANES))
    group = lane // RIM
    pairs = LANES // (2 * RIM)
    spare = [[None] * folded_rows(rows) for _ in range(pairs, count)]
    for block in range(rows // SUB):
        at = pl.ds(block * SUB, SUB)
        planes[count - 2, at, :] = wet_ref[at, :].astype(jnp.float32)
        planes[count - 1, at, :] = cell_ref[at, :].astype(jnp.float32)
        packed = None
        for p in range(count):
            x = planes[p, at, :]
            slot = p if p < pairs else block % pairs
            low, high = turn(x, 2 * RIM * slot), turn(x, 2 * RIM * slot + 2 * RIM)
            old = packed if p < pairs else spare[p - pairs][block // pairs]
            both = jnp.where(group == 2 * slot, low, high)
            new = both if old is None else jnp.where(group // 2 == slot, both, old)
            if p < pairs:
                packed = new
            else:
                spare[p - pairs][block // pairs] = new
        out[at, :] = packed
    start = rows
    for x in [x for p in spare for x in p]:
        out[pl.ds(start, SUB), :] = x
        start += SUB
    strip_rows = strip.shape[0]
    for chunk in range(strip.shape[1] // LANES):
        out[pl.ds(start + chunk * strip_rows, strip_rows), :] = strip_ref[:, chunk * LANES : (chunk + 1) * LANES]
    by_param = [
        [jnp.full((SUB, LANES), param_ref[c, k], jnp.float32) for k in range(fractions)] for c in range(3)
    ]
    for c in range(3):
        each = []
        for k in range(fractions):
            settle, critical, erode = [by_param[n][k] for n in range(3)]
            erode = erode_base * erode
            value = (settle_base * settle, erode / (critical_base * critical), erode)[c]
            coeffs[c, k, :, :] = value
            each.append(value)
        mixed = each[0]
        for k in range(1, fractions):
            mixed = jnp.where(lane // (4 * RIM) == k, each[k], mixed)
        coeffs[c, fractions, :, :] = mixed


def spread_rows(frame_ref, block, shift):
    first = SUB + block * (SUB // 4) + shift
    low = jnp.broadcast_to(frame_ref[pl.ds(first, 1), :], (SUB, LANES))
    high = jnp.broadcast_to(frame_ref[pl.ds(first + 1, 1), :], (SUB, LANES))
    sub = lax.broadcasted_iota(jnp.int32, (SUB, LANES), 0)
    return jnp.where(sub < 4, low, high)


def split_cells(cells, band_cols):
    row = jnp.floor((cells + 0.5) * (1.0 / band_cols))
    return row.astype(jnp.int32), (cells - row * band_cols).astype(jnp.int32)


def row_shift_of(cell_row, block):
    sub = lax.broadcasted_iota(jnp.int32, (SUB, LANES), 0)
    return cell_row - (block * (SUB // 4) + sub // 4)


def lookup(frame_ref, block, shift, column):
    found = pick(spread_rows(frame_ref, block, 0), column)
    below = pick(spread_rows(frame_ref, block, -1), column)
    above = pick(spread_rows(frame_ref, block, 1), column)
    return jnp.where(shift == 0, found, jnp.where(shift < 0, below, above))


def starts_of(col_at, band_cols):
    coarse_start = col_at * (LANES // 4)
    return coarse_start, 0 if band_cols == LANES else coarse_start - (LANES - LANES // 4) // 2


def fill_frame(frame_ref, rows_of):
    frame_ref[...] = jnp.zeros_like(frame_ref)
    for r0, value in rows_of:
        frame_ref[pl.ds(SUB + r0, value.shape[0]), :] = value


def side_maker(geometry, planes, packs, frame_ref):
    band_cols, cols_count = geometry[:2]
    count, rows = planes.shape[:2]
    fractions = count - 5
    col_at = lax.axis_index("col")
    coarse_start, frame_start = starts_of(col_at, band_cols)
    wet_at, cell_at = count - 2, count - 1
    pairs = LANES // (2 * RIM)
    lane = lane_ids((SUB, LANES))
    width = 4 * RIM
    inside = lane % width
    group = lane // width
    is_low = inside < RIM
    is_high = inside >= 3 * RIM
    is_first = inside < 2 * RIM
    has_low = jnp.where(col_at > 0, 1.0, 0.0)
    has_high = jnp.where(col_at < cols_count - 1, 1.0, 0.0)
    scale = jnp.where(is_low, has_low, jnp.where(is_high, has_high, 1.0))
    left = jnp.maximum(col_at - 1, 0)
    right = jnp.minimum(col_at + 1, cols_count - 1)

    def make(block):
        at = pl.ds(block * SUB, SUB)

        def gather_to(p, base):
            if p < pairs:
                source, slot = at, p
            else:
                source = pl.ds(rows + ((p - pairs) * folded_rows(rows) + block // pairs) * SUB, SUB)
                slot = block % pairs
            x = planes[p, at, :]
            low = turn(packs[left, source, :], base - 2 * RIM * slot - RIM)
            high = turn(packs[right, source, :], base + 3 * RIM - 2 * RIM * slot)
            own = jnp.where(is_first, turn(x, base + RIM), turn(x, base + 3 * RIM))
            return jnp.where(is_low, low, jnp.where(is_high, high, own))

        def for_all(p):
            x = gather_to(p, 0)
            x = jnp.where(lane < width, x, pltpu.roll(x, width, 1))
            return jnp.where(lane < 2 * width, x, pltpu.roll(x, 2 * width, 1)) * scale

        sides = [for_all(p) for p in range(3)]
        each = gather_to(3, 0)
        for k in range(1, fractions):
            each = jnp.where(group == k, gather_to(3 + k, k * width), each)
        sides.append(each * scale)
        sides.append(for_all(wet_at))
        side_row, side_col = split_cells(for_all(cell_at), band_cols)
        side_at = jnp.where(scale > 0.0, side_col - frame_start, 0)
        sides.append(lookup(frame_ref, block, row_shift_of(side_row, block), side_at) * scale)
        cell_row, cell_col = split_cells(planes[cell_at, at, :], band_cols)
        shift = row_shift_of(cell_row, block)
        bed = lookup(frame_ref, block, shift, cell_col - frame_start)
        return sides, bed, (shift + 1) * 7 + (cell_col - coarse_start - lane // 4 + 3)

    return make


def edge_kernel(geometry, planes, packs, *refs):
    _, cols_count, strip_rows, from_packs = geometry
    frame = None if from_packs else refs[0]
    send_a, send_b, code, frame_ref = refs[0 if from_packs else 1 :]
    count, rows = planes.shape[:2]
    pairs = LANES // (2 * RIM)
    strip_at = rows + (count - pairs) * folded_rows(rows) * SUB
    if from_packs:
        fill_frame(
            frame_ref, [(d * strip_rows, packs[d, pl.ds(strip_at, strip_rows), :]) for d in range(cols_count)]
        )
    else:
        fill_frame(frame_ref, [(0, frame[...])])
    make = side_maker(geometry, planes, packs, frame_ref)
    parity = lax.axis_index("row") % 2
    last = rows // SUB - 1
    done = [make(0), make(last)]
    for out, turned in ((send_a, parity == 1), (send_b, parity == 0)):
        for p in range(count + 6):
            first, final = [
                planes[p, pl.ds(b * SUB, SUB), :] if p < count - 1 else bed if p == count - 1 else sides[p - count]
                for b, (sides, bed, _) in zip((0, last), done)
            ]
            out[p, :, :] = jnp.where(turned, first, final)
    code[0, :, :] = done[0][2]
    code[1, :, :] = done[1][2]


def half_minmod(before, here, after):
    low = here - before
    high = after - here
    return 0.5 * jnp.maximum(jnp.minimum(low, high), jnp.minimum(jnp.maximum(low, high), 0.0))


def root(x):
    return x * lax.rsqrt(jnp.maximum(x, SMALLEST))


def face_fluxes(lefts, rights, normal, half_open):
    speed_l = lefts[normal] * pl.reciprocal(jnp.maximum(lefts[0], depth_floor))
    speed_r = rights[normal] * pl.reciprocal(jnp.maximum(rights[0], depth_floor))
    wave = jnp.maximum(
        jnp.abs(speed_l) + root(gravity * lefts[0]), jnp.abs(speed_r) + root(gravity * rights[0])
    )
    to_l = half_open * (speed_l + wave)
    to_r = half_open * (speed_r - wave)
    out = [l * to_l + r * to_r for l, r in zip(lefts, rights)]
    out[normal] = out[normal] + (0.5 * gravity) * half_open * (lefts[0] * lefts[0] + rights[0] * rights[0])
    return out


def stepper(
    coeffs, q_main, q_side, static_main, static_side, flux_main, flux_side, exchanged,
    slope_main, slope_side, low_main, high_main, low_side, high_side, cross_main, cross_side,
):
    channels = q_main[0].shape[0]
    fractions = channels - 3
    lane = lane_ids((SUB, LANES))
    width = 4 * RIM
    first_lane = lane == 0
    last_lane = lane == LANES - 1
    wet_at, bed_at = 0, 1

    def coeffs_of(k):
        return [coeffs[c, k, :, :] for c in range(3)]

    def start_of(k):
        return max(k - 3, 0) * width

    def low_edge(x, k):
        return turn(x, 1 - RIM - start_of(k))

    def high_edge(x, k):
        return turn(x, LANES - 1 - 3 * RIM - start_of(k))

    def rows_at(ref, p, row):
        return ref[p, pl.ds(row, SUB), :]

    def statics(block):
        r0 = TOP + block * SUB
        for ref, is_main in ((static_side, False), (static_main, True)):
            w = rows_at(ref, wet_at, r0)
            b_plus = rows_at(ref, bed_at, r0 + 1)
            b_minus = rows_at(ref, bed_at, r0 - 1)
            b = rows_at(ref, bed_at, r0)
            w_right, b_right = pltpu.roll(w, LANES - 1, 1), pltpu.roll(b, LANES - 1, 1)
            b_left = pltpu.roll(b, 1, 1)
            if is_main:
                w_edge, b_edge = rows_at(static_side, wet_at, r0), rows_at(static_side, bed_at, r0)
                w_right = jnp.where(last_lane, high_edge(w_edge, 0), w_right)
                b_right = jnp.where(last_lane, high_edge(b_edge, 0), b_right)
                b_left = jnp.where(first_lane, low_edge(b_edge, 0), b_left)
            at = pl.ds(r0, SUB)
            ref[2, at, :] = 0.5 * (w * rows_at(ref, wet_at, r0 + 1))
            ref[3, at, :] = 0.5 * (w * w_right)
            ref[4, at, :] = (0.5 * gravity) * (b_plus - b_minus)
            ref[5, at, :] = (0.5 * gravity) * (b_right - b_left)
            ref[6, at, :] = time_step * w

    def row_of(block):
        return pl.multiple_of(TOP + block * SUB, SUB)

    def slopes_of(q, s, n, block):
        r0 = row_of(block)
        for k in range(n):
            s[k, pl.ds(r0, SUB), :] = half_minmod(rows_at(q, k, r0 - 1), rows_at(q, k, r0), rows_at(q, k, r0 + 1))

    def row_fluxes(q, s, f, static, n, r0):
        lefts = [rows_at(q, k, r0) + rows_at(s, k, r0) for k in range(n)]
        rights = [rows_at(q, k, r0 + 1) - rows_at(s, k, r0 + 1) for k in range(n)]
        out = face_fluxes(lefts, rights, 1, rows_at(static, 2, r0))
        for k in range(n):
            f[k, pl.ds(r0, SUB), :] = out[k]

    def col_states(here, n, low, high, block, edges):
        at = pl.ds(row_of(block), SUB)
        for k in range(n):
            before, after = pltpu.roll(here[k], 1, 1), pltpu.roll(here[k], LANES - 1, 1)
            if edges is not None:
                before = jnp.where(first_lane, low_edge(edges[min(k, 3)], k), before)
                after = jnp.where(last_lane, high_edge(edges[min(k, 3)], k), after)
            s = half_minmod(before, here[k], after)
            low[k, at, :] = here[k] + s
            high[k, at, :] = here[k] - s

    def col_fluxes(low, high, static, n, r0):
        lefts = [rows_at(low, k, r0) for k in range(n)]
        rights = [pltpu.roll(rows_at(high, k, r0), LANES - 1, 1) for k in range(n)]
        return face_fluxes(lefts, rights, 2, rows_at(static, 3, r0))

    def update(here, net, static, coeffs, r0):
        step = rows_at(static, 6, r0)
        inv = pl.reciprocal(jnp.maximum(here[0], depth_floor))
        u, v = here[1] * inv, here[2] * inv
        squared = u * u + v * v + 1e-06
        drag = drag_coeff * (squared * lax.rsqrt(squared))
        new = [
            here[0] + step * net[0],
            here[1] + step * (net[1] - here[0] * rows_at(static, 4, r0) - drag * u),
            here[2] + step * (net[2] - here[0] * rows_at(static, 5, r0) - drag * v),
        ]
        changes = []
        for k in range(len(here) - 3):
            m = here[3 + k]
            settle, rate, erode = coeffs[k]
            change = step * (settle * m * inv - jnp.maximum(squared * rate - erode, 0.0))
            changes.append(change)
            new.append(m + step * net[3 + k] - change)
        return new, changes


    def slopes(block, level):
        slopes_of(q_main[level % 2], slope_main, channels, block)
        if level < SUBSTEPS - 1:
            slopes_of(q_side[level % 2], slope_side, 4, block)

    def states(block, level):
        r0 = row_of(block)
        edges = [rows_at(q_side[level % 2], k, r0) for k in range(4)]
        here = [rows_at(q_main[level % 2], k, r0) for k in range(channels)]
        col_states(edges, 4, low_side, high_side, block, None)
        col_states(here, channels, low_main, high_main, block, edges)

    def row_faces(block, level):
        r0 = row_of(block)
        row_fluxes(q_main[level % 2], slope_main, flux_main, static_main, channels, r0)
        if level < SUBSTEPS - 1:
            row_fluxes(q_side[level % 2], slope_side, flux_side, static_side, 4, r0)

    def faces(block, level):
        r0 = row_of(block)
        row_faces(block, level)
        for cross, low, high, static, n in (
            (cross_side, low_side, high_side, static_side, 4), (cross_main, low_main, high_main, static_main, channels),
        ):
            for k, f in enumerate(col_fluxes(low, high, static, n, r0)):
                cross[k, pl.ds(r0, SUB), :] = f

    def finish(block, level):
        r0 = row_of(block)
        at = pl.ds(r0, SUB)
        edges = [rows_at(cross_side, k, r0) for k in range(4)]

        def net_of(flux, k, cross, before):
            return (rows_at(flux, k, r0 - 1) - rows_at(flux, k, r0)) + (before - cross)

        if level < SUBSTEPS - 1:
            q = q_side[level % 2]
            net = [net_of(flux_side, k, edges[k], pltpu.roll(edges[k], 1, 1)) for k in range(4)]
            new, _ = update([rows_at(q, k, r0) for k in range(4)], net, static_side, [coeffs_of(fractions)], r0)
            for k in range(4):
                q_side[(level + 1) % 2][k, at, :] = new[k]
        net = []
        for k in range(channels):
            edge = edges[min(k, 3)]
            f = rows_at(cross_main, k, r0)
            before = jnp.where(first_lane, low_edge(edge, k), pltpu.roll(f, 1, 1))
            f = jnp.where(last_lane, turn(edge, LANES - 3 * RIM - start_of(k)), f)
            net.append(net_of(flux_main, k, f, before))
        here = [rows_at(q_main[level % 2], k, r0) for k in range(channels)]
        new, changes = update(here, net, static_main, [coeffs_of(k) for k in range(fractions)], r0)
        for k in range(channels):
            q_main[(level + 1) % 2][k, at, :] = new[k]
        for k in range(fractions):
            if level == 0:
                exchanged[k, at, :] = changes[k]
            else:
                exchanged[k, at, :] = exchanged[k, at, :] + changes[k]

    def first_fluxes(block, level):
        slopes(block, level)
        slopes(block + 1, level)
        row_faces(block, level)

    def each(blocks, level):
        for block in sorted({*blocks, *(b + 1 for b in blocks)}):
            slopes(block, level)
        for stage in (states, faces, finish):
            for block in blocks:
                stage(block, level)

    def sweep(first, end, level):
        size = GROUP if (end - first) % GROUP == 0 else 1
        if end - first <= STRAIGHT or end - first < 3 * size:
            return each(list(range(first, end)), level)

        def of(start):
            return [start + n for n in range(size)]

        def trip(start, carry, ahead=2):
            for block in of(start):
                finish(block, level)
            for block in of(start + 2 * size)[: size if ahead == 2 else ahead]:
                slopes(block, level)
            if ahead:
                for block in of(start + size):
                    faces(block, level)
            if ahead == 2:
                for block in of(start + 2 * size):
                    states(block, level)
            return carry

        for block in range(first, first + 2 * size):
            slopes(block, level)
        for block in of(first):
            states(block, level)
        for block in of(first):
            faces(block, level)
        for block in of(first + size):
            states(block, level)
        trips = (end - first) // size
        lax.fori_loop(0, trips - 2, lambda n, c: trip(first + n * size, c), 0)
        trip(end - 2 * size, 0, ahead=1)
        trip(end - size, 0, ahead=0)

    return statics, first_fluxes, each, sweep


def early_kernel(
    geometry, planes, packs, frame_ref, send_a, send_b, ends, coeffs,
    q_main_a, q_main_b, q_side_a, q_side_b, static_main, static_side, flux_main, flux_side, exchanged, code, *work,
):
    q_main, q_side = (q_main_a, q_main_b), (q_side_a, q_side_b)
    count, rows = planes.shape[:2]
    channels = count - 2
    body = TOP + RIM
    parity = lax.axis_index("row") % 2
    blocks = rows // SUB
    for k in range(channels):
        q_main[0][k, pl.ds(body, rows), :] = planes[k]
    static_main[0, pl.ds(body, rows), :] = planes[channels]
    for block, is_first in ((0, True), (blocks - 1, False)):
        at = pl.ds(body + block * SUB, SUB)
        mine = [
            jnp.where((parity == 1) == is_first, send_a[p], send_b[p]) for p in range(channels + 1, channels + 8)
        ]
        static_main[1, at, :] = mine[0]
        for k in range(4):
            q_side[0][k, at, :] = mine[1 + k]
        static_side[0, at, :] = mine[5]
        static_side[1, at, :] = mine[6]
        code[pl.ds(SUB + block * SUB, SUB), :] = ends[0 if is_first else 1]
    nowhere = jnp.full((SUB, LANES), -1, jnp.int32)
    code[pl.ds(0, SUB), :] = nowhere
    code[pl.ds(SUB + rows, SUB), :] = nowhere
    make = side_maker(geometry, planes, packs, frame_ref)
    for block in range(1, blocks - 1):
        at = pl.ds(body + block * SUB, SUB)
        sides, bed, coded = make(block)
        static_main[1, at, :] = bed
        for k in range(4):
            q_side[0][k, at, :] = sides[k]
        static_side[0, at, :] = sides[4]
        static_side[1, at, :] = sides[5]
        code[pl.ds(SUB + block * SUB, SUB), :] = coded
    statics, first_fluxes, each, sweep = stepper(
        coeffs, q_main, q_side, static_main, static_side, flux_main, flux_side, exchanged, *work
    )
    total = blocks + 2
    for block in range(1, total - 2):
        statics(block)
    for level in range(AHEAD):
        first_fluxes(1 + level, level)
        sweep(2 + level, total - 2 - level, level)


def late_kernel(
    band_cols, recv_a, recv_b, coeffs, code,
    q_in_0, q_in_1, q_in_2, q_in_3, static_main_in, static_side_in, flux_main_in, flux_side_in, exchanged_in,
    depth_out, flow_out, mud_out, partial,
    q_main_a, q_main_b, q_side_a, q_side_b, static_main, static_side, flux_main, flux_side, exchanged,
    sems, *work,
):
    q_main, q_side = (q_main_a, q_main_b), (q_side_a, q_side_b)
    del q_in_0, q_in_1, q_in_2, q_in_3, static_main_in, static_side_in, flux_main_in, flux_side_in, exchanged_in
    rows = code.shape[0] - 2 * SUB
    channels = q_main[0].shape[0]
    fractions = channels - 3
    body = TOP + RIM
    parity = lax.axis_index("row") % 2
    total = rows // SUB + 2

    def fill(put, p):
        a, b = recv_a[p], recv_b[p]
        put(pl.ds(TOP, RIM), jnp.where(parity == 1, a, b))
        put(pl.ds(body + rows, RIM), jnp.where(parity == 1, b, a))

    for k in range(channels + 8):
        def put(at, x, k=k):
            if k < channels:
                q_main[0][k, at, :] = x
            elif k < channels + 2:
                static_main[k - channels, at, :] = x
            elif k < channels + 6:
                q_side[0][k - channels - 2, at, :] = x
            else:
                static_side[k - channels - 6, at, :] = x

        fill(put, k)
    statics, first_fluxes, each, sweep = stepper(
        coeffs, q_main, q_side, static_main, static_side, flux_main, flux_side, exchanged, *work
    )
    for block in (0, total - 2, total - 1):
        statics(block)
    if total > 3:
        statics(1)
    for level in range(SUBSTEPS):
        if level < AHEAD:
            each([*range(2 + level), *range(total - 2 - level, total)], level)
        elif level < SUBSTEPS - 1:
            sweep(0, total, level)
        else:
            first_fluxes(0, level)
            sweep(1, total - 1, level)
    final = q_main[SUBSTEPS % 2]
    here = pl.ds(body, rows)
    copies = [pltpu.make_async_copy(final.at[0, here], depth_out, sems.at[0])]
    copies.append(pltpu.make_async_copy(final.at[pl.ds(1, 2), here], flow_out, sems.at[1]))
    copies.append(pltpu.make_async_copy(final.at[pl.ds(3, fractions), here], mud_out, sems.at[2]))
    for copy in copies:
        copy.start()

    coarse_rows = rows // 4
    def apart(ref, first, row_shift):
        return [ref[pl.ds(first - 4 * row_shift + k, coarse_rows, stride=4), :] for k in range(4)]

    codes = [apart(code, SUB, row_shift - 1) for row_shift in range(3)]
    to_coarse = (
        lax.broadcasted_iota(jnp.int32, (LANES, LANES), 0) // 4 == lax.broadcasted_iota(jnp.int32, (LANES, LANES), 1)
    ).astype(jnp.bfloat16)
    coarse_start, frame_start = starts_of(lax.axis_index("col"), band_cols)
    moved_total = None
    for col_shift in range(7):
        sums = [None] * fractions
        for row_shift in range(3):
            hits = [c == row_shift * 7 + col_shift for c in codes[row_shift]]
            for f in range(fractions):
                for hit, x in zip(hits, apart(exchanged.at[f], body, row_shift - 1)):
                    x = jnp.where(hit, x, 0.0)
                    sums[f] = x if sums[f] is None else sums[f] + x
        rest = jnp.concatenate(sums, axis=0)
        z = None
        for _ in range(2):
            term = rest.astype(jnp.bfloat16)
            rest = rest - term.astype(jnp.float32)
            moved = jnp.dot(term, to_coarse, preferred_element_type=jnp.float32)
            z = moved if z is None else z + moved
        z = pltpu.roll(z, (coarse_start - frame_start + col_shift - 3 + LANES) % LANES, 1)
        moved_total = z if moved_total is None else moved_total + z
    partial[...] = moved_total
    for copy in copies:
        copy.wait()


def bed_kernel(geometry, sums, bed, planes, bed_out, deposit_out, fine, frame_ref, total_ref):
    band_cols, cols_count, strip_rows = geometry
    cells = planes.at[planes.shape[0] - 1]
    rows = cells.shape[0]
    band_rows = rows // 4
    fractions = sums.shape[1] // band_rows
    total = sums[0]
    for d in range(1, cols_count):
        total = total + sums[d]
    total_ref[...] = (exner_factor / 16.0) * total
    at = lax.axis_index("col") * strip_rows
    frame_ref[...] = jnp.zeros_like(frame_ref)
    whole = None
    for f in range(fractions):
        part = total_ref[pl.ds(f * band_rows, band_rows), :]
        whole = part if whole is None else whole + part
        deposit_out[f, :, :] = total_ref[pl.ds(f * band_rows + at, strip_rows), :]
    frame_ref[pl.ds(SUB, band_rows), :] = bed[pl.ds(SUB, band_rows), :] + whole
    bed_out[...] = frame_ref[pl.ds(SUB + at, strip_rows), :]
    for block in range(rows // SUB):
        here = pl.ds(block * SUB, SUB)
        cell_row, cell_col = split_cells(cells[here, :], band_cols)
        fine[here, :] = lookup(frame_ref, block, row_shift_of(cell_row, block), cell_col)


def local(water_depth, discharge, sediment, bed_level, cell_map, wet_mask, sediment_params):
    tile_rows, tile_cols = water_depth.shape
    fractions = sediment.shape[0]
    strip_rows, band_cols = bed_level.shape
    cols_count = lax.axis_size("col")
    rows_count = lax.axis_size("row")
    band_rows = tile_rows // 4
    f32 = functools.partial(jax.ShapeDtypeStruct, dtype=jnp.float32)
    narrow = band_cols == LANES
    col_at = lax.axis_index("col")
    frame_start = starts_of(col_at, band_cols)[1]
    chunks = band_cols // LANES
    extra = (5 + fractions - LANES // (2 * RIM)) * folded_rows(tile_rows) * SUB
    pack_rows = tile_rows + extra + -(-chunks * strip_rows // SUB) * SUB

    channels = 3 + fractions
    count = channels + 2
    space = functools.partial(pltpu.VMEM, dtype=jnp.float32)
    arguments = (water_depth, discharge, sediment, wet_mask, cell_map, bed_level, sediment_params)
    planes, coeffs, packed = pl.pallas_call(
        pack_kernel,
        out_shape=(
            f32((count, tile_rows, LANES)), f32((3, fractions + 1, SUB, LANES)), f32((pack_rows, LANES)),
        ),
        in_specs=[hbm()] * 7, out_specs=(vmem(),) * 3, compiler_params=params_of(),
        scratch_shapes=[
            pltpu.VMEM((tile_rows, LANES), jnp.int32), pltpu.VMEM((tile_rows, LANES), jnp.int32),
            space(bed_level.shape), pltpu.SMEM(sediment_params.shape, jnp.float32), pltpu.SemaphoreType.DMA((7,)),
        ],
    )(*[pltpu.with_memory_space_constraint(x, pltpu.HBM) for x in arguments])
    packs = lax.all_gather(packed, "col", axis=0)

    frames = []
    if not narrow:
        strips = packs[:, tile_rows + extra : tile_rows + extra + chunks * strip_rows]
        band = strips.reshape(cols_count, chunks, strip_rows, LANES).transpose(0, 2, 1, 3).reshape(band_rows, band_cols)
        wide = jnp.pad(band, ((0, 0), (LANES, LANES)))
        frames = [lax.dynamic_slice(wide, (jnp.int32(0), frame_start + LANES), (band_rows, LANES))]
    geometry = (band_cols, cols_count, strip_rows, narrow)
    send_a, send_b, ends, framed = pl.pallas_call(
        functools.partial(edge_kernel, geometry),
        out_shape=(
            f32((count + 6, SUB, LANES)), f32((count + 6, SUB, LANES)),
            jax.ShapeDtypeStruct((2, SUB, LANES), jnp.int32), f32((band_rows + 2 * SUB, LANES)),
        ),
        in_specs=[vmem()] * (2 + len(frames)), out_specs=(vmem(),) * 4, compiler_params=params_of(),
    )(planes, packs, *frames)

    pairs_a = [p for i in range(0, rows_count - 1, 2) for p in ((i, i + 1), (i + 1, i))]
    pairs_b = [p for i in range(1, rows_count - 1, 2) for p in ((i, i + 1), (i + 1, i))]
    recv_a = lax.ppermute(send_a, "row", pairs_a)
    recv_b = lax.ppermute(send_b, "row", pairs_b)

    span = tile_rows + 2 * RIM + 3 * SUB
    state = (
        f32((channels, span, LANES)), f32((channels, span, LANES)), f32((4, span, LANES)), f32((4, span, LANES)),
        f32((7, span, LANES)), f32((7, span, LANES)),
        f32((channels, span, LANES)), f32((4, span, LANES)), f32((fractions, span, LANES)),
    )
    main_space, side_space = space((channels, span, LANES)), space((4, span, LANES))
    work_space = [main_space, side_space, main_space, main_space, side_space, side_space, main_space, side_space]
    *begun, code = pl.pallas_call(
        functools.partial(early_kernel, geometry),
        out_shape=(*state, jax.ShapeDtypeStruct((tile_rows + 2 * SUB, LANES), jnp.int32)),
        in_specs=[vmem()] * 7, out_specs=(vmem(),) * 10, compiler_params=params_of(), scratch_shapes=work_space,
    )(planes, packs, framed, send_a, send_b, ends, coeffs)
    depth_out, discharge_out, sediment_out, partial = pl.pallas_call(
        functools.partial(late_kernel, band_cols),
        out_shape=(
            f32(water_depth.shape), f32(discharge.shape), f32(sediment.shape), f32((fractions * band_rows, LANES)),
            *state,
        ),
        in_specs=[vmem()] * 13, out_specs=(hbm(),) * 3 + (vmem(),) * 10, compiler_params=params_of(),
        input_output_aliases={4 + k: 4 + k for k in range(9)},
        scratch_shapes=[pltpu.SemaphoreType.DMA((3,)), *work_space],
    )(recv_a, recv_b, coeffs, code, *begun)[:4]

    sums = lax.all_gather(partial, "col", axis=0)
    geometry = (band_cols if narrow else LANES, cols_count, strip_rows)
    if narrow:
        look_cells = planes
    else:
        wide = jnp.zeros((fractions, band_rows, band_cols + 2 * LANES), jnp.float32)
        for d in range(cols_count):
            start = LANES + d * (tile_cols // 4) - (LANES - tile_cols // 4) // 2
            wide = wide.at[:, :, start : start + LANES].add(sums[d].reshape(fractions, band_rows, LANES))
        share = lax.dynamic_slice_in_dim(wide, col_at * strip_rows, strip_rows, axis=1)[:, :, LANES:-LANES]
        deposit_wide = exner_factor / 16.0 * share
        bed_wide = bed_level + jnp.sum(deposit_wide, axis=0)
        sums = lax.dynamic_slice_in_dim(wide, frame_start + LANES, LANES, axis=2).reshape(1, -1, LANES)
        geometry = (LANES, 1, strip_rows)
        look_cells = (cell_map // band_cols * LANES + cell_map % band_cols - frame_start).astype(jnp.float32)[None]
    bed_new, deposit, fine_bed = pl.pallas_call(
        functools.partial(bed_kernel, geometry),
        out_shape=(f32((strip_rows, LANES)), f32((fractions, strip_rows, LANES)), f32((tile_rows, LANES))),
        in_specs=[vmem()] * 3, out_specs=(vmem(),) * 3, compiler_params=params_of(),
        scratch_shapes=[space((band_rows + 2 * SUB, LANES)), space((fractions * band_rows, LANES))],
    )(sums, framed, look_cells)
    if not narrow:
        bed_new, deposit = bed_wide, deposit_wide
    return (depth_out, discharge_out, sediment_out, fine_bed, bed_new, deposit)


def solution(mesh):
    placed = (
        P("row", "col"),
        P(None, "row", "col"),
        P(None, "row", "col"),
        P(("row", "col"), None),
        P("row", "col"),
        P("row", "col"),
        P(),
    )
    return jax.shard_map(
        local,
        mesh=mesh,
        in_specs=placed,
        out_specs=(
            P("row", "col"),
            P(None, "row", "col"),
            P(None, "row", "col"),
            P("row", "col"),
            P(("row", "col"), None),
            P(None, ("row", "col"), None),
        ),
        check_vma=False,
    )
```

```python
import functools

import jax
import jax.numpy as jnp
from jax import lax
from jax.experimental import pallas as pl
from jax.experimental.pallas import tpu as pltpu
from jax.sharding import PartitionSpec as P


SUBSTEPS = 4
LANES = 128
SUB = 8
GROUP = 1
STRAIGHT = 12
AHEAD = 3
TOP = SUB
SMALLEST = 1.1754944e-38
RIM = 2 * SUBSTEPS

gravity = 1.0
time_step = 0.2
depth_floor = 1.25
drag_coeff = 0.02
settle_base = 0.05
critical_base = 0.05
erode_base = 0.002
exner_factor = 400.0


def vmem():
    return pl.BlockSpec(memory_space=pltpu.VMEM)


def lane_ids(shape):
    return lax.broadcasted_iota(jnp.int32, shape, len(shape) - 1)


def params_of(limit=16 << 20):
    return pltpu.CompilerParams(vmem_limit_bytes=limit)


def pick(table, index):
    return jnp.take_along_axis(table, index, axis=1, mode="promise_in_bounds")


def hbm():
    return pl.BlockSpec(memory_space=pltpu.HBM)


def turn(x, shift):
    shift = shift % LANES
    return pltpu.roll(x, shift, 1) if shift else x


def folded_rows(rows):
    return -(-rows // SUB // (LANES // (2 * RIM)))


def pack_kernel(depth, flow, mud, wet, cells, strip, params, planes, coeffs, out, wet_ref, cell_ref, strip_ref, param_ref, sems):
    rows = depth.shape[0]
    fractions = mud.shape[0]
    moves = [
        (depth, planes.at[0]), (flow, planes.at[pl.ds(1, 2)]), (mud, planes.at[pl.ds(3, fractions)]), (wet, wet_ref),
        (cells, cell_ref), (strip, strip_ref), (params, param_ref),
    ]
    copies = [pltpu.make_async_copy(src, dst, sems.at[k]) for k, (src, dst) in enumerate(moves)]
    for copy in copies:
        copy.start()
    for copy in copies:
        copy.wait()
    count = 5 + fractions
    lane = lane_ids((SUB, LANES))
    group = lane // RIM
    pairs = LANES // (2 * RIM)
    spare = [[None] * folded_rows(rows) for _ in range(pairs, count)]
    for block in range(rows // SUB):
        at = pl.ds(block * SUB, SUB)
        planes[count - 2, at, :] = wet_ref[at, :].astype(jnp.float32)
        planes[count - 1, at, :] = cell_ref[at, :].astype(jnp.float32)
        packed = None
        for p in range(count):
            x = planes[p, at, :]
            slot = p if p < pairs else block % pairs
            low, high = turn(x, 2 * RIM * slot), turn(x, 2 * RIM * slot + 2 * RIM)
            old = packed if p < pairs else spare[p - pairs][block // pairs]
            both = jnp.where(group == 2 * slot, low, high)
            new = both if old is None else jnp.where(group // 2 == slot, both, old)
            if p < pairs:
                packed = new
            else:
                spare[p - pairs][block // pairs] = new
        out[at, :] = packed
    start = rows
    for x in [x for p in spare for x in p]:
        out[pl.ds(start, SUB), :] = x
        start += SUB
    strip_rows = strip.shape[0]
    for chunk in range(strip.shape[1] // LANES):
        out[pl.ds(start + chunk * strip_rows, strip_rows), :] = strip_ref[:, chunk * LANES : (chunk + 1) * LANES]
    by_param = [
        [jnp.full((SUB, LANES), param_ref[c, k], jnp.float32) for k in range(fractions)] for c in range(3)
    ]
    for c in range(3):
        each = []
        for k in range(fractions):
            settle, critical, erode = [by_param[n][k] for n in range(3)]
            erode = erode_base * erode
            value = (settle_base * settle, erode / (critical_base * critical), erode)[c]
            coeffs[c, k, :, :] = value
            each.append(value)
        mixed = each[0]
        for k in range(1, fractions):
            mixed = jnp.where(lane // (4 * RIM) == k, each[k], mixed)
        coeffs[c, fractions, :, :] = mixed


WINDOW_LOW = 5
WINDOW = LANES // 4 + 2 * WINDOW_LOW


def fill_window(window_ref, frame_ref, first):
    rows = window_ref.shape[0]
    lane = lane_ids((rows, LANES))
    parts = [
        pltpu.roll(frame_ref[pl.ds(SUB - 1 + n, rows), :], (n * WINDOW - first + 2 * LANES) % LANES, 1)
        for n in range(3)
    ]
    window_ref[...] = jnp.where(lane < WINDOW, parts[0], jnp.where(lane < 2 * WINDOW, parts[1], parts[2]))


def split_cells(cells, band_cols):
    row = jnp.floor((cells + 0.5) * (1.0 / band_cols))
    return row.astype(jnp.int32), (cells - row * band_cols).astype(jnp.int32)


def row_shift_of(cell_row, block):
    sub = lax.broadcasted_iota(jnp.int32, (SUB, LANES), 0)
    return cell_row - (block * (SUB // 4) + sub // 4)


def lookup(window_ref, block, shift, column):
    first = block * (SUB // 4)
    low = jnp.broadcast_to(window_ref[pl.ds(first, 1), :], (SUB, LANES))
    high = jnp.broadcast_to(window_ref[pl.ds(first + 1, 1), :], (SUB, LANES))
    sub = lax.broadcasted_iota(jnp.int32, (SUB, LANES), 0)
    return pick(jnp.where(sub < 4, low, high), (shift + 1) * WINDOW + column)


def starts_of(col_at, band_cols):
    coarse_start = col_at * (LANES // 4)
    return coarse_start, 0 if band_cols == LANES else coarse_start - (LANES - LANES // 4) // 2


def fill_frame(frame_ref, rows_of):
    frame_ref[...] = jnp.zeros_like(frame_ref)
    for r0, value in rows_of:
        frame_ref[pl.ds(SUB + r0, value.shape[0]), :] = value


def side_maker(geometry, planes, packs, window_ref):
    band_cols, cols_count = geometry[:2]
    count, rows = planes.shape[:2]
    fractions = count - 5
    col_at = lax.axis_index("col")
    coarse_start = starts_of(col_at, band_cols)[0]
    wet_at, cell_at = count - 2, count - 1
    pairs = LANES // (2 * RIM)
    lane = lane_ids((SUB, LANES))
    width = 4 * RIM
    inside = lane % width
    group = lane // width
    is_low = inside < RIM
    is_high = inside >= 3 * RIM
    is_first = inside < 2 * RIM
    has_low = jnp.where(col_at > 0, 1.0, 0.0)
    has_high = jnp.where(col_at < cols_count - 1, 1.0, 0.0)
    scale = jnp.where(is_low, has_low, jnp.where(is_high, has_high, 1.0))
    left = jnp.maximum(col_at - 1, 0)
    right = jnp.minimum(col_at + 1, cols_count - 1)

    def gather_to(block, p, base):
        at = pl.ds(block * SUB, SUB)
        if p < pairs:
            source, slot = at, p
        else:
            source = pl.ds(rows + ((p - pairs) * folded_rows(rows) + block // pairs) * SUB, SUB)
            slot = block % pairs
        x = planes[p, at, :]
        low = turn(packs[left, source, :], base - 2 * RIM * slot - RIM)
        high = turn(packs[right, source, :], base + 3 * RIM - 2 * RIM * slot)
        own = jnp.where(is_first, turn(x, base + RIM), turn(x, base + 3 * RIM))
        return jnp.where(is_low, low, jnp.where(is_high, high, own))

    def gathered(block, order):
        out = gather_to(block, order[0], 0)
        for k, p in enumerate(order[1:], 1):
            out = jnp.where(group == k, gather_to(block, p, k * width), out)
        return out * scale

    def packed(block):
        each = gathered(block, [3 + k for k in range(fractions)])
        return each, gathered(block, (0, 1, 2, wet_at)), gathered(block, (cell_at,))

    def cells_of(block, first_group):
        cells = first_group
        for k in range(1, LANES // width):
            cells = jnp.where(group == k, pltpu.roll(first_group, k * width, 1), cells)
        side_row, side_col = split_cells(cells, band_cols)
        inside_grid = scale > 0.0
        side_shift = jnp.where(inside_grid, row_shift_of(side_row, block), 0)
        side_at = jnp.where(inside_grid, side_col - coarse_start + WINDOW_LOW, 0)
        cell_row, cell_col = split_cells(planes[cell_at, pl.ds(block * SUB, SUB), :], band_cols)
        return side_shift, side_at, row_shift_of(cell_row, block), cell_col - coarse_start

    def beds(block, cells):
        side_shift, side_at, shift, column = cells
        side_bed = lookup(window_ref, block, side_shift, side_at) * scale
        bed = lookup(window_ref, block, shift, column + WINDOW_LOW)
        return side_bed, bed, (shift + 1) * 7 + (column - lane // 4 + 3)

    def make(blocks):
        first = [packed(block) for block in blocks]
        second = [cells_of(block, x[2]) for block, x in zip(blocks, first)]
        third = [beds(block, x) for block, x in zip(blocks, second)]
        return [(each, shared, side_bed, bed, code) for (each, shared, _), (side_bed, bed, code) in zip(first, third)]

    return make


def edge_kernel(geometry, planes, packs, *refs):
    _, cols_count, strip_rows, from_packs = geometry
    frame = None if from_packs else refs[0]
    send_a, send_b, code, frame_ref, window_ref = refs[0 if from_packs else 1 :]
    count, rows = planes.shape[:2]
    pairs = LANES // (2 * RIM)
    strip_at = rows + (count - pairs) * folded_rows(rows) * SUB
    if from_packs:
        fill_frame(
            frame_ref, [(d * strip_rows, packs[d, pl.ds(strip_at, strip_rows), :]) for d in range(cols_count)]
        )
    else:
        fill_frame(frame_ref, [(0, frame[...])])
    coarse_start, frame_start = starts_of(lax.axis_index("col"), geometry[0])
    fill_window(window_ref, frame_ref, coarse_start - frame_start - WINDOW_LOW)
    make = side_maker(geometry, planes, packs, window_ref)
    parity = lax.axis_index("row") % 2
    last = rows // SUB - 1
    done = make((0, last))
    for out, turned in ((send_a, parity == 1), (send_b, parity == 0)):
        for p in range(count + 3):
            first, final = [
                planes[p, pl.ds(b * SUB, SUB), :] if p < count - 1 else bed if p == count - 1 else (each, shared, side_bed)[p - count]
                for b, (each, shared, side_bed, bed, _) in zip((0, last), done)
            ]
            out[p, :, :] = jnp.where(turned, first, final)
    code[0, :, :] = done[0][4]
    code[1, :, :] = done[1][4]


def half_minmod(before, here, after):
    low = here - before
    high = after - here
    return 0.5 * jnp.maximum(jnp.minimum(low, high), jnp.minimum(jnp.maximum(low, high), 0.0))


def root(x):
    return x * lax.rsqrt(jnp.maximum(x, SMALLEST))


def face_fluxes(lefts, rights, normal, half_open):
    speed_l = lefts[normal] * pl.reciprocal(jnp.maximum(lefts[0], depth_floor))
    speed_r = rights[normal] * pl.reciprocal(jnp.maximum(rights[0], depth_floor))
    wave = jnp.maximum(
        jnp.abs(speed_l) + root(gravity * lefts[0]), jnp.abs(speed_r) + root(gravity * rights[0])
    )
    to_l = half_open * (speed_l + wave)
    to_r = half_open * (speed_r - wave)
    out = [l * to_l + r * to_r for l, r in zip(lefts, rights)]
    out[normal] = out[normal] + (0.5 * gravity) * half_open * (lefts[0] * lefts[0] + rights[0] * rights[0])
    return out


def stepper(
    coeffs, q_main, q_side, static_main, static_side, flux_main, flux_side, exchanged,
    slope_main, slope_side, low_main, high_main, low_side, high_side, cross_main, cross_side,
):
    channels = q_main[0].shape[0]
    fractions = channels - 3
    lane = lane_ids((SUB, LANES))
    width = 4 * RIM
    first_lane = lane == 0
    last_lane = lane == LANES - 1
    wet_at, bed_at = 0, 1
    rim_block = (exchanged.shape[1] - 4 * SUB) // SUB

    def coeffs_of(k):
        return [coeffs[c, k, :, :] for c in range(3)]

    def start_of(k):
        return max(k - 3, 0) * width

    def low_edge(x, k):
        return turn(x, 1 - RIM - start_of(k))

    def high_edge(x, k):
        return turn(x, LANES - 1 - 3 * RIM - start_of(k))

    def rows_at(ref, p, row):
        return ref[p, pl.ds(row, SUB), :]

    def statics(block):
        r0 = TOP + block * SUB
        for ref, is_main in ((static_side, False), (static_main, True)):
            w = rows_at(ref, wet_at, r0)
            b_plus = rows_at(ref, bed_at, r0 + 1)
            b_minus = rows_at(ref, bed_at, r0 - 1)
            b = rows_at(ref, bed_at, r0)
            w_right, b_right = pltpu.roll(w, LANES - 1, 1), pltpu.roll(b, LANES - 1, 1)
            b_left = pltpu.roll(b, 1, 1)
            if is_main:
                w_edge, b_edge = rows_at(static_side, wet_at, r0), rows_at(static_side, bed_at, r0)
                w_right = jnp.where(last_lane, high_edge(w_edge, 0), w_right)
                b_right = jnp.where(last_lane, high_edge(b_edge, 0), b_right)
                b_left = jnp.where(first_lane, low_edge(b_edge, 0), b_left)
            at = pl.ds(r0, SUB)
            ref[2, at, :] = 0.5 * (w * rows_at(ref, wet_at, r0 + 1))
            ref[3, at, :] = 0.5 * (w * w_right)
            ref[4, at, :] = (0.5 * gravity) * (b_plus - b_minus)
            ref[5, at, :] = (0.5 * gravity) * (b_right - b_left)
            ref[6, at, :] = time_step * w

    def row_of(block):
        return pl.multiple_of(TOP + block * SUB, SUB)

    def slopes_of(q, s, n, block):
        r0 = row_of(block)
        for k in range(n):
            s[k, pl.ds(r0, SUB), :] = half_minmod(rows_at(q, k, r0 - 1), rows_at(q, k, r0), rows_at(q, k, r0 + 1))

    def row_fluxes(q, s, f, static, n, r0):
        lefts = [rows_at(q, k, r0) + rows_at(s, k, r0) for k in range(n)]
        rights = [rows_at(q, k, r0 + 1) - rows_at(s, k, r0 + 1) for k in range(n)]
        out = face_fluxes(lefts, rights, 1, rows_at(static, 2, r0))
        for k in range(n):
            f[k, pl.ds(r0, SUB), :] = out[k]

    def col_states(here, n, low, high, block, edges):
        at = pl.ds(row_of(block), SUB)
        for k in range(n):
            before, after = pltpu.roll(here[k], 1, 1), pltpu.roll(here[k], LANES - 1, 1)
            if edges is not None:
                before = jnp.where(first_lane, low_edge(edges[min(k, 3)], k), before)
                after = jnp.where(last_lane, high_edge(edges[min(k, 3)], k), after)
            s = half_minmod(before, here[k], after)
            low[k, at, :] = here[k] + s
            high[k, at, :] = here[k] - s

    def col_fluxes(low, high, static, n, r0):
        lefts = [rows_at(low, k, r0) for k in range(n)]
        rights = [pltpu.roll(rows_at(high, k, r0), LANES - 1, 1) for k in range(n)]
        return face_fluxes(lefts, rights, 2, rows_at(static, 3, r0))

    def update(here, net, static, coeffs, r0):
        step = rows_at(static, 6, r0)
        inv = pl.reciprocal(jnp.maximum(here[0], depth_floor))
        u, v = here[1] * inv, here[2] * inv
        squared = u * u + v * v + 1e-06
        drag = drag_coeff * (squared * lax.rsqrt(squared))
        new = [
            here[0] + step * net[0],
            here[1] + step * (net[1] - here[0] * rows_at(static, 4, r0) - drag * u),
            here[2] + step * (net[2] - here[0] * rows_at(static, 5, r0) - drag * v),
        ]
        changes = []
        for k in range(len(here) - 3):
            m = here[3 + k]
            settle, rate, erode = coeffs[k]
            change = step * (settle * m * inv - jnp.maximum(squared * rate - erode, 0.0))
            changes.append(change)
            new.append(m + step * net[3 + k] - change)
        return new, changes


    def slopes(block, level):
        slopes_of(q_main[level % 2], slope_main, channels, block)
        if level < SUBSTEPS - 1:
            slopes_of(q_side[level % 2], slope_side, 4, block)

    def states(block, level):
        r0 = row_of(block)
        edges = [rows_at(q_side[level % 2], k, r0) for k in range(4)]
        here = [rows_at(q_main[level % 2], k, r0) for k in range(channels)]
        col_states(edges, 4, low_side, high_side, block, None)
        col_states(here, channels, low_main, high_main, block, edges)

    def row_faces(block, level):
        r0 = row_of(block)
        row_fluxes(q_main[level % 2], slope_main, flux_main, static_main, channels, r0)
        if level < SUBSTEPS - 1:
            row_fluxes(q_side[level % 2], slope_side, flux_side, static_side, 4, r0)

    def faces(block, level):
        r0 = row_of(block)
        row_faces(block, level)
        for cross, low, high, static, n in (
            (cross_side, low_side, high_side, static_side, 4), (cross_main, low_main, high_main, static_main, channels),
        ):
            for k, f in enumerate(col_fluxes(low, high, static, n, r0)):
                cross[k, pl.ds(r0, SUB), :] = f

    def finish(block, level):
        r0 = row_of(block)
        at = pl.ds(r0, SUB)
        edges = [rows_at(cross_side, k, r0) for k in range(4)]

        def net_of(flux, k, cross, before):
            return (rows_at(flux, k, r0 - 1) - rows_at(flux, k, r0)) + (before - cross)

        if level < SUBSTEPS - 1:
            q = q_side[level % 2]
            net = [net_of(flux_side, k, edges[k], pltpu.roll(edges[k], 1, 1)) for k in range(4)]
            new, _ = update([rows_at(q, k, r0) for k in range(4)], net, static_side, [coeffs_of(fractions)], r0)
            for k in range(4):
                q_side[(level + 1) % 2][k, at, :] = new[k]
        net = []
        for k in range(channels):
            edge = edges[min(k, 3)]
            f = rows_at(cross_main, k, r0)
            before = jnp.where(first_lane, low_edge(edge, k), pltpu.roll(f, 1, 1))
            f = jnp.where(last_lane, turn(edge, LANES - 3 * RIM - start_of(k)), f)
            net.append(net_of(flux_main, k, f, before))
        here = [rows_at(q_main[level % 2], k, r0) for k in range(channels)]
        new, changes = update(here, net, static_main, [coeffs_of(k) for k in range(fractions)], r0)
        for k in range(channels):
            q_main[(level + 1) % 2][k, at, :] = new[k]
        for k in range(fractions if 0 < block < rim_block else 0):
            if level == 0:
                exchanged[k, at, :] = changes[k]
            else:
                exchanged[k, at, :] = exchanged[k, at, :] + changes[k]

    def first_fluxes(block, level):
        slopes(block, level)
        slopes(block + 1, level)
        row_faces(block, level)

    def each(work, meanwhile=()):
        def all_slopes(some):
            for block, level in sorted({*some, *((b + 1, n) for b, n in some)}):
                slopes(block, level)

        def run(stage, some):
            for block, level in some:
                stage(block, level)

        all_slopes(work)
        run(states, work)
        run(faces, work)
        if meanwhile:
            first_fluxes(meanwhile[0][0] - 1, meanwhile[0][1])
            all_slopes(meanwhile)
            run(states, meanwhile)
        run(finish, work)
        run(faces, meanwhile)
        run(finish, meanwhile)

    def sweep(first, end, level):
        size = GROUP if (end - first) % GROUP == 0 else 1
        if end - first <= STRAIGHT or end - first < 3 * size:
            return each([(block, level) for block in range(first, end)])

        def of(start):
            return [start + n for n in range(size)]

        def trip(start, carry, ahead=2):
            for block in of(start):
                finish(block, level)
            for block in of(start + 2 * size)[: size if ahead == 2 else ahead]:
                slopes(block, level)
            if ahead:
                for block in of(start + size):
                    faces(block, level)
            if ahead == 2:
                for block in of(start + 2 * size):
                    states(block, level)
            return carry

        for block in range(first, first + 2 * size):
            slopes(block, level)
        for block in of(first):
            states(block, level)
        for block in of(first):
            faces(block, level)
        for block in of(first + size):
            states(block, level)
        trips = (end - first) // size
        lax.fori_loop(0, trips - 2, lambda n, c: trip(first + n * size, c), 0)
        trip(end - 2 * size, 0, ahead=1)
        trip(end - size, 0, ahead=0)

    return statics, first_fluxes, each, sweep


def put_sides(q, static, at, each, shared, bed):
    group = lane_ids(shared.shape) // (4 * RIM)
    turned = [shared] + [pltpu.roll(shared, 4 * RIM * n, 1) for n in range(1, 4)]
    for k, (ref, p) in enumerate(((q, 0), (q, 1), (q, 2), (static, 0))):
        x = turned[(0 - k) % 4]
        for g in range(1, 4):
            x = jnp.where(group == g, turned[(g - k) % 4], x)
        ref[p, at, :] = x
    q[3, at, :] = each
    static[1, at, :] = bed


def early_kernel(
    geometry, planes, packs, window_ref, send_a, send_b, ends, coeffs,
    q_main_a, q_main_b, q_side_a, q_side_b, static_main, static_side, flux_main, flux_side, exchanged, code, *work,
):
    q_main, q_side = (q_main_a, q_main_b), (q_side_a, q_side_b)
    count, rows = planes.shape[:2]
    channels = count - 2
    body = TOP + RIM
    parity = lax.axis_index("row") % 2
    blocks = rows // SUB
    for k in range(channels):
        q_main[0][k, pl.ds(body, rows), :] = planes[k]
    static_main[0, pl.ds(body, rows), :] = planes[channels]
    for block, is_first in ((0, True), (blocks - 1, False)):
        at = pl.ds(body + block * SUB, SUB)
        mine = [
            jnp.where((parity == 1) == is_first, send_a[p], send_b[p]) for p in range(channels + 1, channels + 5)
        ]
        static_main[1, at, :] = mine[0]
        put_sides(q_side[0], static_side, at, *mine[1:])
        code[pl.ds(SUB + block * SUB, SUB), :] = ends[0 if is_first else 1]
    nowhere = jnp.full((SUB, LANES), -1, jnp.int32)
    code[pl.ds(0, SUB), :] = nowhere
    code[pl.ds(SUB + rows, SUB), :] = nowhere
    make = side_maker(geometry, planes, packs, window_ref)
    inner = range(1, blocks - 1)
    for block, (each, shared, side_bed, bed, coded) in zip(inner, make(inner)):
        at = pl.ds(body + block * SUB, SUB)
        static_main[1, at, :] = bed
        put_sides(q_side[0], static_side, at, each, shared, side_bed)
        code[pl.ds(SUB + block * SUB, SUB), :] = coded
    statics, first_fluxes, each, sweep = stepper(
        coeffs, q_main, q_side, static_main, static_side, flux_main, flux_side, exchanged, *work
    )
    total = blocks + 2
    for block in range(1, total - 2):
        statics(block)
    for level in range(AHEAD):
        first_fluxes(1 + level, level)
        sweep(2 + level, total - 2 - level, level)


def late_kernel(
    band_cols, recv_a, recv_b, coeffs, code,
    q_in_0, q_in_1, q_in_2, q_in_3, static_main_in, static_side_in, flux_main_in, flux_side_in, exchanged_in,
    depth_out, flow_out, mud_out, partial,
    q_main_a, q_main_b, q_side_a, q_side_b, static_main, static_side, flux_main, flux_side, exchanged,
    sems, *work,
):
    q_main, q_side = (q_main_a, q_main_b), (q_side_a, q_side_b)
    del q_in_0, q_in_1, q_in_2, q_in_3, static_main_in, static_side_in, flux_main_in, flux_side_in, exchanged_in
    rows = code.shape[0] - 2 * SUB
    channels = q_main[0].shape[0]
    fractions = channels - 3
    body = TOP + RIM
    parity = lax.axis_index("row") % 2
    total = rows // SUB + 2

    for at, turned in ((pl.ds(TOP, RIM), parity == 1), (pl.ds(body + rows, RIM), parity == 0)):
        came = [jnp.where(turned, recv_a[p], recv_b[p]) for p in range(channels + 5)]
        for k in range(channels):
            q_main[0][k, at, :] = came[k]
        for k in range(2):
            static_main[k, at, :] = came[channels + k]
        put_sides(q_side[0], static_side, at, *came[channels + 2 :])
    statics, first_fluxes, each, sweep = stepper(
        coeffs, q_main, q_side, static_main, static_side, flux_main, flux_side, exchanged, *work
    )
    for block in (0, total - 2, total - 1):
        statics(block)
    if total > 3:
        statics(1)

    def outer(level):
        return [(block, level) for block in (*range(2 + level), *range(total - 2 - level, total))]

    each(outer(0), [(block, AHEAD) for block in range(2 + AHEAD, total - 2 - AHEAD)] if AHEAD < SUBSTEPS - 1 else ())
    for level in range(1, SUBSTEPS - 1):
        if level <= AHEAD:
            each(outer(level))
        else:
            sweep(0, total, level)
    first_fluxes(0, SUBSTEPS - 1)
    sweep(1, total - 1, SUBSTEPS - 1)
    final = q_main[SUBSTEPS % 2]
    here = pl.ds(body, rows)
    copies = [pltpu.make_async_copy(final.at[0, here], depth_out, sems.at[0])]
    copies.append(pltpu.make_async_copy(final.at[pl.ds(1, 2), here], flow_out, sems.at[1]))
    copies.append(pltpu.make_async_copy(final.at[pl.ds(3, fractions), here], mud_out, sems.at[2]))
    for copy in copies:
        copy.start()

    coarse_rows = rows // 4

    def apart(ref, first, row_shift):
        return [ref[pl.ds(first - 4 * row_shift + k, coarse_rows, stride=4), :] for k in range(4)]

    codes = [apart(code, SUB, row_shift - 1) for row_shift in range(3)]
    to_coarse = (
        lax.broadcasted_iota(jnp.int32, (LANES, LANES), 0) // 4 == lax.broadcasted_iota(jnp.int32, (LANES, LANES), 1)
    ).astype(jnp.bfloat16)
    coarse_start, frame_start = starts_of(lax.axis_index("col"), band_cols)
    moved_total = None
    for col_shift in range(7):
        sums = [None] * fractions
        for row_shift in range(3):
            hits = [c == row_shift * 7 + col_shift for c in codes[row_shift]]
            for f in range(fractions):
                for hit, x in zip(hits, apart(exchanged.at[f], body, row_shift - 1)):
                    x = jnp.where(hit, x, 0.0)
                    sums[f] = x if sums[f] is None else sums[f] + x
        rest = jnp.concatenate(sums, axis=0)
        z = None
        for _ in range(2):
            term = rest.astype(jnp.bfloat16)
            rest = rest - term.astype(jnp.float32)
            moved = jnp.dot(term, to_coarse, preferred_element_type=jnp.float32)
            z = moved if z is None else z + moved
        z = pltpu.roll(z, (coarse_start - frame_start + col_shift - 3 + LANES) % LANES, 1)
        moved_total = z if moved_total is None else moved_total + z
    partial[...] = moved_total
    for copy in copies:
        copy.wait()


def bed_kernel(geometry, sums, bed, planes, bed_out, deposit_out, fine, frame_ref, total_ref, window_ref):
    band_cols, cols_count, strip_rows = geometry
    cells = planes.at[planes.shape[0] - 1]
    rows = cells.shape[0]
    band_rows = rows // 4
    fractions = sums.shape[1] // band_rows
    total = sums[0]
    for d in range(1, cols_count):
        total = total + sums[d]
    total_ref[...] = (exner_factor / 16.0) * total
    at = lax.axis_index("col") * strip_rows
    frame_ref[...] = jnp.zeros_like(frame_ref)
    whole = None
    for f in range(fractions):
        part = total_ref[pl.ds(f * band_rows, band_rows), :]
        whole = part if whole is None else whole + part
        deposit_out[f, :, :] = total_ref[pl.ds(f * band_rows + at, strip_rows), :]
    frame_ref[pl.ds(SUB, band_rows), :] = bed[pl.ds(SUB, band_rows), :] + whole
    bed_out[...] = frame_ref[pl.ds(SUB + at, strip_rows), :]
    coarse_start, frame_start = starts_of(lax.axis_index("col"), band_cols)
    fill_window(window_ref, frame_ref, coarse_start - frame_start - WINDOW_LOW)
    for block in range(rows // SUB):
        here = pl.ds(block * SUB, SUB)
        cell_row, cell_col = split_cells(cells[here, :], band_cols)
        fine[here, :] = lookup(window_ref, block, row_shift_of(cell_row, block), cell_col - coarse_start + WINDOW_LOW)


def local(water_depth, discharge, sediment, bed_level, cell_map, wet_mask, sediment_params):
    tile_rows, tile_cols = water_depth.shape
    fractions = sediment.shape[0]
    strip_rows, band_cols = bed_level.shape
    cols_count = lax.axis_size("col")
    rows_count = lax.axis_size("row")
    band_rows = tile_rows // 4
    f32 = functools.partial(jax.ShapeDtypeStruct, dtype=jnp.float32)
    narrow = band_cols == LANES
    col_at = lax.axis_index("col")
    frame_start = starts_of(col_at, band_cols)[1]
    chunks = band_cols // LANES
    extra = (5 + fractions - LANES // (2 * RIM)) * folded_rows(tile_rows) * SUB
    pack_rows = tile_rows + extra + -(-chunks * strip_rows // SUB) * SUB

    channels = 3 + fractions
    count = channels + 2
    space = functools.partial(pltpu.VMEM, dtype=jnp.float32)
    arguments = (water_depth, discharge, sediment, wet_mask, cell_map, bed_level, sediment_params)
    planes, coeffs, packed = pl.pallas_call(
        pack_kernel,
        out_shape=(
            f32((count, tile_rows, LANES)), f32((3, fractions + 1, SUB, LANES)), f32((pack_rows, LANES)),
        ),
        in_specs=[hbm()] * 7, out_specs=(vmem(),) * 3, compiler_params=params_of(),
        scratch_shapes=[
            pltpu.VMEM((tile_rows, LANES), jnp.int32), pltpu.VMEM((tile_rows, LANES), jnp.int32),
            space(bed_level.shape), pltpu.SMEM(sediment_params.shape, jnp.float32), pltpu.SemaphoreType.DMA((7,)),
        ],
    )(*[pltpu.with_memory_space_constraint(x, pltpu.HBM) for x in arguments])
    packs = lax.all_gather(packed, "col", axis=0)

    frames = []
    if not narrow:
        strips = packs[:, tile_rows + extra : tile_rows + extra + chunks * strip_rows]
        band = strips.reshape(cols_count, chunks, strip_rows, LANES).transpose(0, 2, 1, 3).reshape(band_rows, band_cols)
        wide = jnp.pad(band, ((0, 0), (LANES, LANES)))
        frames = [lax.dynamic_slice(wide, (jnp.int32(0), frame_start + LANES), (band_rows, LANES))]
    geometry = (band_cols, cols_count, strip_rows, narrow)
    send_a, send_b, ends, framed, window = pl.pallas_call(
        functools.partial(edge_kernel, geometry),
        out_shape=(
            f32((count + 3, SUB, LANES)), f32((count + 3, SUB, LANES)),
            jax.ShapeDtypeStruct((2, SUB, LANES), jnp.int32), f32((band_rows + 2 * SUB, LANES)),
            f32((band_rows, LANES)),
        ),
        in_specs=[vmem()] * (2 + len(frames)), out_specs=(vmem(),) * 5, compiler_params=params_of(),
    )(planes, packs, *frames)

    pairs_a = [p for i in range(0, rows_count - 1, 2) for p in ((i, i + 1), (i + 1, i))]
    pairs_b = [p for i in range(1, rows_count - 1, 2) for p in ((i, i + 1), (i + 1, i))]
    recv_b = lax.ppermute(send_b, "row", pairs_b)
    recv_a = lax.ppermute(send_a, "row", pairs_a)

    span = tile_rows + 2 * RIM + 3 * SUB
    state = (
        f32((channels, span, LANES)), f32((channels, span, LANES)), f32((4, span, LANES)), f32((4, span, LANES)),
        f32((7, span, LANES)), f32((7, span, LANES)),
        f32((channels, span, LANES)), f32((4, span, LANES)), f32((fractions, span, LANES)),
    )
    main_space, side_space = space((channels, span, LANES)), space((4, span, LANES))
    work_space = [main_space, side_space, main_space, main_space, side_space, side_space, main_space, side_space]
    *begun, code = pl.pallas_call(
        functools.partial(early_kernel, geometry),
        out_shape=(*state, jax.ShapeDtypeStruct((tile_rows + 2 * SUB, LANES), jnp.int32)),
        in_specs=[vmem()] * 7, out_specs=(vmem(),) * 10, compiler_params=params_of(), scratch_shapes=work_space,
    )(planes, packs, window, send_a, send_b, ends, coeffs)
    depth_out, discharge_out, sediment_out, partial = pl.pallas_call(
        functools.partial(late_kernel, band_cols),
        out_shape=(
            f32(water_depth.shape), f32(discharge.shape), f32(sediment.shape), f32((fractions * band_rows, LANES)),
            *state,
        ),
        in_specs=[vmem()] * 13, out_specs=(hbm(),) * 3 + (vmem(),) * 10, compiler_params=params_of(),
        input_output_aliases={4 + k: 4 + k for k in range(9)},
        scratch_shapes=[pltpu.SemaphoreType.DMA((3,)), *work_space],
    )(recv_a, recv_b, coeffs, code, *begun)[:4]

    sums = lax.all_gather(partial, "col", axis=0)
    geometry = (band_cols, cols_count, strip_rows)
    if not narrow:
        wide = jnp.zeros((fractions, band_rows, band_cols + 2 * LANES), jnp.float32)
        for d in range(cols_count):
            start = LANES + d * (tile_cols // 4) - (LANES - tile_cols // 4) // 2
            wide = wide.at[:, :, start : start + LANES].add(sums[d].reshape(fractions, band_rows, LANES))
        share = lax.dynamic_slice_in_dim(wide, col_at * strip_rows, strip_rows, axis=1)[:, :, LANES:-LANES]
        deposit_wide = exner_factor / 16.0 * share
        bed_wide = bed_level + jnp.sum(deposit_wide, axis=0)
        sums = lax.dynamic_slice_in_dim(wide, frame_start + LANES, LANES, axis=2).reshape(1, -1, LANES)
        geometry = (band_cols, 1, strip_rows)
    bed_new, deposit, fine_bed = pl.pallas_call(
        functools.partial(bed_kernel, geometry),
        out_shape=(f32((strip_rows, LANES)), f32((fractions, strip_rows, LANES)), f32((tile_rows, LANES))),
        in_specs=[vmem()] * 3, out_specs=(vmem(),) * 3, compiler_params=params_of(),
        scratch_shapes=[
            space((band_rows + 2 * SUB, LANES)), space((fractions * band_rows, LANES)), space((band_rows, LANES)),
        ],
    )(sums, framed, planes)
    if not narrow:
        bed_new, deposit = bed_wide, deposit_wide
    return (depth_out, discharge_out, sediment_out, fine_bed, bed_new, deposit)


def solution(mesh):
    placed = (
        P("row", "col"),
        P(None, "row", "col"),
        P(None, "row", "col"),
        P(("row", "col"), None),
        P("row", "col"),
        P("row", "col"),
        P(),
    )
    return jax.shard_map(
        local,
        mesh=mesh,
        in_specs=placed,
        out_specs=(
            P("row", "col"),
            P(None, "row", "col"),
            P(None, "row", "col"),
            P("row", "col"),
            P(("row", "col"), None),
            P(None, ("row", "col"), None),
        ),
        check_vma=False,
    )
```
